512 devices in a mesh: gx: 16 (over x, y_lo, core), gy: 32 (over y_hi, z).
Axes of the slice: x: 4, y: 4 (y_hi: 2, y_lo: 2; y = y_hi * 2 + y_lo), z: 16, core: 2. Of those that a mesh axis runs over, the one named last changes fastest.
Arguments:
- plate_motion: bfloat16 [32, 64, 128, 2, 128], P('gx', 'gy'), may hold values from -6 to 6
- adjoint_load: bfloat16 [32, 64, 128, 2, 128], P('gx', 'gy'), may hold values from -6 to 6
- excitation: bfloat16 [32, 64, 128, 2, 128], P('gx', 'gy'), may hold values from -6 to 6
- coupling: bfloat16 [32, 64, 5, 2, 128, 128], P('gx', 'gy'), may hold values from -0.25 to 0.25
- joints: int32 [32, 64, 4], P('gx', 'gy'), may hold values 0 or 1
- hydro: bfloat16 [2, 16384, 16384], P(None, 'gx', 'gy'), may hold values from -0.046875 to 0.046875
- panel_map: bfloat16 [16384, 2, 2, 128], P(('gx', 'gy')), may hold values from -0.25 to 0.25
Outputs:
- residual: float32 [32, 64, 128, 2, 128], P('gx', 'gy')
- multiplier: float32 [32, 64, 128, 2, 128], P('gx', 'gy')
- sensitivity: float32 [32, 64], P('gx', 'gy')
The draws below stay inside these ranges and needn't reach their ends.
All inputs are finite; a program needn't handle non-finite values. No bound on the sum of `joints` on one device may be relied on, other than what follows from the above.
Results may differ from the reference program's by a relative error of at most 0.0031.
Values may be sent and summed in bfloat16 or wider, within the bound.
A program may use at most 64 MiB of HBM per device.

```python
import math
import jax
import jax.numpy as jnp
from jax import lax

NDOF = 128
BX = 2
BY = 2
NH = 128
PD = 32
GBX = 32
GBY = 64
NP = 16384
N_GX = 16
N_GY = 32
DEVICES = 512


def with_ends(entries, rng, least, high):
    longest = entries.shape.index(max(entries.shape))
    spots = []
    for shift in (0, 1):
        where = [jax.random.randint(jax.random.fold_in(rng, axis), (), 0, length) for axis, length in enumerate(entries.shape)]
        where[longest] = (where[longest] + shift) % entries.shape[longest]
        spots.append(tuple(where))
    return entries.at[spots[0]].set(least).at[spots[1]].set(high)


def levels(key, extent, shards, least, top_value):
    loudness = 1.0
    for axis_at, parts in shards:
        draws = jax.random.uniform(jax.random.fold_in(jax.random.fold_in(key, 6), axis_at), (parts,), jnp.float32, least / len(shards), top_value / len(shards))
        loudness = loudness * jnp.repeat(jnp.exp(draws), extent[axis_at] // parts).reshape((-1,) + (1,) * (len(extent) - 1 - axis_at))
    return loudness


def normal_values(rng, extent, deviation, most, split=(), kind=jnp.bfloat16):
    loudness = levels(rng, extent, split, -0.22, 0.18) if split else 1.0
    values = jax.random.normal(rng, extent, jnp.float32) * deviation * loudness
    return jnp.minimum(jnp.maximum(values, -most), most).astype(kind)


def setup_inputs(seed: int = 0) -> dict:
    splits = jax.random.split(jax.random.key(seed), 8)
    return {
        "plate_motion": normal_values(splits[0], (GBX, GBY, NH, 2, NDOF), 1.0, 6.0, ((0, 16), (1, 32))),
        "adjoint_load": normal_values(splits[1], (GBX, GBY, NH, 2, NDOF), 1.0, 6.0, ((0, 16), (1, 32))),
        "excitation": normal_values(splits[2], (GBX, GBY, NH, 2, NDOF), 1.0, 6.0, ((0, 16), (1, 32))),
        "coupling": normal_values(splits[3], (GBX, GBY, 5, 2, NDOF, NDOF), (5 * NDOF) ** -0.5, 0.25, ((0, 16), (1, 32))),
        "joints": with_ends((jax.random.randint(splits[4], (GBX, GBY, 4), 0, 4) < 3).astype(jnp.int32), jax.random.fold_in(splits[4], 1), 0, 1),
        "hydro": normal_values(splits[5], (2, NP, NP), NP ** -0.5, 0.046875, ((1, 16), (2, 32))),
        "panel_map": normal_values(splits[6], (NP, BX, BY, NDOF), (BX * BY * NDOF) ** -0.5, 0.25, ((0, 512),)),
    }


def complex_apply(form, coupling, vector):
    real_c = coupling[..., 0, :, :].astype(jnp.float32)
    imag_c = coupling[..., 1, :, :].astype(jnp.float32)
    real_v = vector[..., 0, :].astype(jnp.float32)
    imag_v = vector[..., 1, :].astype(jnp.float32)
    first = jnp.einsum(form, real_c, real_v) - jnp.einsum(form, imag_c, imag_v)
    second = jnp.einsum(form, real_c, imag_v) + jnp.einsum(form, imag_c, real_v)
    return jnp.stack([first, second], axis=-2)

def adjoint_apply(form, coupling, vector):
    real_c = coupling[..., 0, :, :].astype(jnp.float32)
    imag_c = coupling[..., 1, :, :].astype(jnp.float32)
    real_v = vector[..., 0, :].astype(jnp.float32)
    imag_v = vector[..., 1, :].astype(jnp.float32)
    first = jnp.einsum(form, real_c, real_v) + jnp.einsum(form, imag_c, imag_v)
    second = jnp.einsum(form, real_c, imag_v) - jnp.einsum(form, imag_c, real_v)
    return jnp.stack([first, second], axis=-2)

def neighbour(field, off_x, off_y):
    widths = ((1, 1), (1, 1)) + ((0, 0),) * (field.ndim - 2)
    padded = jnp.pad(field, widths)
    return padded[1 + off_x:1 + off_x + GBX, 1 + off_y:1 + off_y + GBY]

def to_tiles(field):
    rest = field.shape[2:]
    shaped = field.reshape((N_GX, BX, N_GY, BY) + rest).swapaxes(1, 2)
    return shaped.reshape((DEVICES, BX, BY) + rest)

def from_tiles(field):
    rest = field.shape[3:]
    shaped = field.reshape((N_GX, N_GY, BX, BY) + rest).swapaxes(1, 2)
    return shaped.reshape((GBX, GBY) + rest)

def reference(plate_motion, adjoint_load, excitation, coupling, joints, hydro, panel_map):
    offsets = ((-1, 0), (1, 0), (0, -1), (0, 1))
    links = joints.astype(jnp.float32)
    own = complex_apply('xyij,xyhj->xyhi', coupling[:, :, 0], plate_motion)
    structural = own
    for direction in range(4):
        moved = neighbour(plate_motion, offsets[direction][0], offsets[direction][1])
        term = complex_apply('xyij,xyhj->xyhi', coupling[:, :, direction + 1], moved)
        structural = structural + links[:, :, direction, None, None, None] * term
    adjoint_part = adjoint_apply('xyji,xyhj->xyhi', coupling[:, :, 0], adjoint_load)
    for direction in range(4):
        term = adjoint_apply('xyji,xyhj->xyhi', coupling[:, :, direction + 1], adjoint_load)
        term = links[:, :, direction, None, None, None] * term
        adjoint_part = adjoint_part + neighbour(term, -offsets[direction][0], -offsets[direction][1])
    lift = math.sqrt(BX * BY * NDOF / PD)
    map_tiles = panel_map.reshape(DEVICES, PD, BX, BY, NDOF).astype(jnp.float32)
    motion_panels = jnp.einsum('dnxyk,dxyhck->cdnh', map_tiles, to_tiles(plate_motion).astype(jnp.float32))
    motion_panels = motion_panels.astype(jnp.bfloat16).reshape(2, NP, NH)
    load_panels = jnp.einsum('dnxyk,dxyhck->cdnh', map_tiles, to_tiles(adjoint_load).astype(jnp.float32))
    load_panels = load_panels.astype(jnp.bfloat16).reshape(2, NP, NH)
    column_order = motion_panels.reshape(2, N_GX, N_GY, PD, NH).swapaxes(1, 2).reshape(2, NP, NH)
    band = N_GY * PD

    def band_matrix(index):
        return lax.dynamic_slice_in_dim(hydro, index * band, band, 1)

    def band_forward(index):
        masked = band_matrix(index)
        first = jnp.dot(masked[0], column_order[0], preferred_element_type=jnp.float32) - jnp.dot(masked[1], column_order[1], preferred_element_type=jnp.float32)
        second = jnp.dot(masked[0], column_order[1], preferred_element_type=jnp.float32) + jnp.dot(masked[1], column_order[0], preferred_element_type=jnp.float32)
        return jnp.stack([first, second])
    indices = jnp.arange(N_GX).astype(jnp.int32)
    pressure = lax.map(band_forward, indices).transpose(1, 0, 2, 3).reshape(2, NP, NH).astype(jnp.bfloat16)

    def band_adjoint(carry, index):
        masked = band_matrix(index)
        loads = lax.dynamic_slice_in_dim(load_panels, index * band, band, 1)
        first = jnp.dot(masked[0].T, loads[0], preferred_element_type=jnp.float32) + jnp.dot(masked[1].T, loads[1], preferred_element_type=jnp.float32)
        second = jnp.dot(masked[0].T, loads[1], preferred_element_type=jnp.float32) - jnp.dot(masked[1].T, loads[0], preferred_element_type=jnp.float32)
        return (carry + jnp.stack([first, second]), None)
    reaction, unused = lax.scan(band_adjoint, jnp.zeros((2, NP, NH), jnp.float32), indices)
    reaction = reaction.reshape(2, N_GY, N_GX, PD, NH).swapaxes(1, 2).reshape(2, NP, NH).astype(jnp.bfloat16)
    pressure_force = jnp.einsum('dnxyk,cdnh->dxyhck', map_tiles, pressure.reshape(2, DEVICES, PD, NH).astype(jnp.float32))
    reaction_force = jnp.einsum('dnxyk,cdnh->dxyhck', map_tiles, reaction.reshape(2, DEVICES, PD, NH).astype(jnp.float32))
    residual = structural + lift * from_tiles(pressure_force) - excitation.astype(jnp.float32)
    multiplier = adjoint_part + lift * from_tiles(reaction_force)
    sensitivity = lax.optimization_barrier(jnp.sum(multiplier * own, axis=(2, 3, 4))) / math.sqrt(NH * NDOF)
    return (residual, multiplier, sensitivity)
```

```python
import functools
import math

import jax
import jax.numpy as jnp
from jax import lax
from jax.experimental import pallas as pl
from jax.experimental.pallas import tpu as pltpu
from jax.sharding import PartitionSpec as P

MESH = pl.DeviceIdType.MESH
F32 = jnp.float32
BF16 = jnp.bfloat16
NGX, NGY, NZ = 16, 32, 16
PD = 32
FAR = 5
CHUNKS = (0, FAR, NZ - FAR)


def nn(a, b):
    return jnp.dot(a, b, preferred_element_type=F32)


def nt(a, b):
    return lax.dot_general(a, b, (((1,), (1,)), ((), ())), preferred_element_type=F32)


def tn(a, b):
    return lax.dot_general(a, b, (((0,), (0,)), ((), ())), preferred_element_type=F32)


def times_i(x):
    rows = x.shape[0]
    even = lax.rem(lax.broadcasted_iota(jnp.int32, x.shape, 0), 2) == 0
    return jnp.where(even, -pltpu.roll(x, rows - 1, 0), pltpu.roll(x, 1, 0))


def lane_i(width):
    r = lax.broadcasted_iota(jnp.int32, (width, width), 0)
    c = lax.broadcasted_iota(jnp.int32, (width, width), 1)
    odd = lax.rem(c, 2) == 1
    plus = jnp.where(jnp.logical_and(odd, r == c - 1), 1.0, 0.0)
    minus = jnp.where(jnp.logical_and(jnp.logical_not(odd), r == c + 1), 1.0, 0.0)
    return (plus - minus).astype(BF16)


def kernel(
    joints, plate_h, adj_h, exc_h, coup_h, hyd_h, pmap_h,
    res_h, mult_h, own_h, pressure_o, reaction_o, map_o,
    X, A, JA, E, C, H, HT, PM, PM32, MG, MP, LG, LP, PO, PB, YB, SB, RA, TB, RB, QB, RG,
    HX, HY, TX, TY, RX, RY, RES, MULT, OWN,
    lsem, gx_s, gx_r, fa_s, fa_r, nb_s, nb_r, yf_s, yf_r, yx_s, yx_r,
    ra_s, ra_r, rb_s, rb_r, rx_s, rx_r, h_s, h_r,
):
    gx = lax.axis_index("gx")
    gy = lax.axis_index("gy")
    yh = lax.div(gy, NZ)
    z = lax.rem(gy, NZ)

    def gx_at(r):
        return lax.rem(gx + r, NGX)

    def gy_at(dz, dy):
        return lax.rem(yh + dy, 2) * NZ + lax.rem(z + dz, NZ)

    def near(q):
        return lax.rem(lax.rem(q + 2, 5) - 2 + NZ, NZ)

    def each(lo, hi, f):
        def body(i, carry):
            f(i)
            return carry
        lax.fori_loop(lo, hi, body, 0)

    def remote(src, dst, send, recv, where):
        return pltpu.make_async_remote_copy(
            src, dst, send, recv, device_id=where, device_id_type=MESH)

    loads = [
        pltpu.make_async_copy(s, d, lsem.at[i])
        for i, (s, d) in enumerate(
            ((pmap_h, PM), (adj_h, A), (plate_h, X), (coup_h, C), (hyd_h, H), (exc_h, E))
        )
    ]
    for c in loads:
        c.start()

    bar = pltpu.get_barrier_semaphore()

    def greet(x, y):
        pl.semaphore_signal(bar, inc=1, device_id=(x, y), device_id_type=MESH)

    for dz in (FAR, NZ - FAR, 3, NZ - 3):
        greet(gx, gy_at(dz, 0))
    greet(gx, gy_at(0, 1))
    for step in (1, NGY - 1):
        greet(gx, lax.rem(gy + step, NGY))
    each(1, 5, lambda q: greet(gx, gy_at(near(q), 0)))
    each(1, NGX, lambda r: greet(gx_at(r), gy))

    def far_gather(i):
        return remote(LG.at[gy], LG.at[gy], fa_s.at[i], fa_r.at[i],
                      (gx, gy_at((FAR, NZ - FAR)[i], 0)))

    def far_gather_in(i):
        slot = gy_at((NZ - FAR, FAR)[i], 0)
        return remote(LG.at[slot], LG.at[slot], fa_s.at[i], fa_r.at[i], (gx, slot))

    def gather(r):
        return remote(MG.at[gx], MG.at[gx], gx_s.at[r], gx_r.at[r], (gx_at(r), gy))

    def gather_in(r):
        slot = gx_at(NGX - r)
        return remote(MG.at[slot], MG.at[slot], gx_s.at[r], gx_r.at[r], (slot, gy))

    def near_gather(q, c):
        slot = gy_at(CHUNKS[c], 0)
        return remote(LG.at[slot], LG.at[slot], nb_s.at[q, c], nb_r.at[q, c],
                      (gx, gy_at(near(q), 0)))

    def near_slot(q, c):
        return lax.rem(NZ - near(q) + CHUNKS[c], NZ)

    def near_gather_in(q, c):
        slot = gy_at(near_slot(q, c), 0)
        return remote(LG.at[slot], LG.at[slot], nb_s.at[q, c], nb_r.at[q, c], (gx, slot))

    def opposite_gather():
        slot = gy_at(NZ - FAR, 0)
        return remote(LG.at[slot], LG.at[slot], nb_s.at[0, 0], nb_r.at[0, 0], (gx, gy_at(3, 0)))

    def opposite_gather_in():
        slot = gy_at(8, 0)
        return remote(LG.at[slot], LG.at[slot], nb_s.at[0, 0], nb_r.at[0, 0], (gx, slot))

    def across(o):
        slot = gy_at(o, 0)
        return remote(LG.at[slot], LG.at[slot], yf_s.at[o], yf_r.at[o], (gx, gy_at(0, 1)))

    def across_in(o):
        slot = gy_at(o, 1)
        return remote(LG.at[slot], LG.at[slot], yf_s.at[o], yf_r.at[o], (gx, gy_at(0, 1)))

    def swap(t):
        rows = pl.ds(t * 8, 8)
        return remote(PB.at[rows], YB.at[rows], yx_s.at[t], yx_r.at[t], (gx, gy_at(0, 1)))

    def near_part(q, c):
        return remote(SB.at[lax.rem(z + near(q) + CHUNKS[c], NZ)], RA.at[q, c],
                      ra_s.at[q, c], ra_r.at[q, c], (gx, gy_at(near(q), 0)))

    def opposite_part():
        return remote(SB.at[lax.rem(z + 8, NZ)], RA.at[0, 0],
                      ra_s.at[0, 0], ra_r.at[0, 0], (gx, gy_at(3, 0)))

    def far_part(i):
        return remote(TB.at[i], RB.at[i], rb_s.at[i], rb_r.at[i],
                      (gx, gy_at((FAR, NZ - FAR)[i], 0)))

    def sum_part(r):
        return remote(QB.at[gx_at(r)], RG.at[r], rx_s.at[r], rx_r.at[r], (gx_at(r), gy))

    def halo_x(src, dst, k, s):
        return remote(src.at[s], dst.at[1 - s], h_s.at[k, s], h_r.at[k, 1 - s],
                      (gx_at(1 if s else NGX - 1), gy))

    def halo_y(src, dst, k, s):
        return remote(src.at[:, s] if k == 1 else src.at[s], dst.at[1 - s],
                      h_s.at[k, s], h_r.at[k, 1 - s],
                      (gx, lax.rem(gy + (1 if s else NGY - 1), NGY)))

    loads[0].wait()
    PM32[...] = PM[...].astype(F32)
    for b in range(4):
        map_o[:, b * 128:(b + 1) * 128] = PM32[pl.ds(b, PD, stride=4), :].astype(BF16)

    def panels(V):
        total = nt(map_o[:, 0:128], V[0, 0])
        for b in range(1, 4):
            total = total + nt(map_o[:, b * 128:(b + 1) * 128], V[b // 2, b % 2])
        return total.astype(BF16)

    loads[1].wait()
    LG[gy] = panels(A)
    loads[2].wait()
    MG[gx] = panels(X)

    pl.semaphore_wait(bar, 4 + 1 + 2 + 4 + 15)

    for i in range(2):
        far_gather(i).start()
    each(1, NGX, lambda r: gather(r).start())
    across(0).start()
    each(1, 5, lambda q: near_gather(q, 0).start())

    loads[3].wait()

    def link(bx, by, d):
        return joints[bx, by, d].astype(F32)

    def edge_x(bx):
        v = gx + 2 * bx - 1
        return jnp.where(jnp.logical_and(v >= 0, v < NGX), 1.0, 0.0).astype(F32)

    def edge_y(by):
        v = gy + 2 * by - 1
        return jnp.where(jnp.logical_and(v >= 0, v < NGY), 1.0, 0.0).astype(F32)

    def back(bx, by, d):
        m = (bx * 2 + by) * 5 + d
        return nn(A[bx, by], C[m, 0]) - nn(JA[bx, by], C[m, 1])

    def outgoing(b):
        bx, by = lax.div(b, 2), lax.rem(b, 2)
        JA[bx, by] = times_i(A[bx, by].astype(F32)).astype(BF16)
        TX[bx, by] = (link(bx, by, bx) * edge_x(bx) * back(bx, by, 1 + bx)).astype(BF16)
        TY[by, bx] = (link(bx, by, 2 + by) * edge_y(by) * back(bx, by, 3 + by)).astype(BF16)

    each(0, 4, outgoing)
    loads[4].wait()
    jm = lane_i(256)

    def turn(t):
        rows = pl.ds(pl.multiple_of(t * 256, 256), 256)
        for c in range(2):
            HT[c, t] = H[c, rows, :].T

    each(0, 2, turn)

    each(1, NGX, lambda r: gather_in(r).wait_recv())
    MP[...] = nn(MG[...].reshape(NGX * PD, 256), jm).astype(BF16)

    def press(y, t):
        rows = pl.ds(pl.multiple_of(y * 512 + t * 256, 256), 256)
        p = nn(H[0, rows, :], MG[...].reshape(NGX * PD, 256)) + nn(H[1, rows, :], MP[...])
        return p.reshape(8, PD, 256)

    def press_other(t):
        PB[pl.ds(t * 8, 8)] = press(1 - yh, t).astype(BF16)
        swap(t).start()

    def press_own(t):
        PO[pl.ds(t * 8, 8)] = press(yh, t)

    each(0, 2, press_other)

    far_gather_in(0).wait_recv()
    opposite_gather().start()
    each(1, 5, lambda q: near_gather(q, 2).start())
    across(NZ - FAR).start()
    far_gather_in(1).wait_recv()
    each(1, 5, lambda q: near_gather(q, 1).start())
    across(FAR).start()

    each(0, 2, press_own)
    for s in range(2):
        halo_x(X, HX, 0, s).start()
        halo_y(X, HY, 1, s).start()
    for s in range(2):
        halo_x(TX, RX, 2, s).start()
        halo_y(TY, RY, 3, s).start()
    each(2, 4, turn)

    def local_forward(b):
        bx, by = lax.div(b, 2), lax.rem(b, 2)
        m = b * 5
        x = X[bx, by]
        own = nt(x, C[m, 0]) + times_i(nt(x, C[m, 1]))
        OWN[bx, by] = own
        dx, dy = 1 - bx, 3 - by
        fx, fy = link(bx, by, dx), link(bx, by, dy)
        xs, ys = X[1 - bx, by], X[bx, 1 - by]
        re = fx * nt(xs, C[m + 1 + dx, 0]) + fy * nt(ys, C[m + 1 + dy, 0])
        im = fx * nt(xs, C[m + 1 + dx, 1]) + fy * nt(ys, C[m + 1 + dy, 1])
        RES[bx, by] = own + re + times_i(im) - E[bx, by].astype(F32)

    def local_adjoint(b):
        bx, by = lax.div(b, 2), lax.rem(b, 2)
        MULT[bx, by] = (
            back(bx, by, 0)
            + link(1 - bx, by, bx) * back(1 - bx, by, 1 + bx)
            + link(bx, 1 - by, 2 + by) * back(bx, 1 - by, 3 + by))

    each(0, 4, local_adjoint)

    opposite_gather_in().wait_recv()
    across(8).start()

    def pass_on(c):
        def go(q):
            near_gather_in(q, c).wait_recv()
            across(near_slot(q, c)).start()
        each(1, 5, go)

    pass_on(0)
    pass_on(2)
    pass_on(1)

    each(0, 2, lambda t: swap(t).wait_recv())

    def add_other(t):
        PO[t] = PO[t] + YB[t].astype(F32)
        SB[t] = PO[t].astype(BF16)

    each(0, NZ, add_other)
    opposite_part().start()

    def start_parts(q):
        for c in (1, 2, 0):
            near_part(q, c).start()

    each(1, 5, start_parts)

    def turn_loads(k):
        LP[k] = nn(LG[pl.ds(k * 8, 8)].reshape(256, 256), jm).astype(BF16)

    def react(y, t):
        rows = pl.ds(pl.multiple_of(t * 256, 256), 256)
        total = jnp.zeros((256, 256), F32)
        for i in range(2):
            k = 2 * y + i
            total = total + nn(HT[0, k, rows, :], LG[pl.ds(k * 8, 8)].reshape(256, 256))
            total = total - nn(HT[1, k, rows, :], LP[k])
        return total.reshape(8, PD, 256)

    def react_own(t):
        QB[pl.ds(t * 8, 8)] = react(yh, t)

    def react_other(t):
        rows = pl.ds(t * 8, 8)
        QB[rows] = QB[rows] + react(1 - yh, t)

    each(2 * yh, 2 * yh + 2, turn_loads)
    each(0, 2, react_own)
    each(0, NZ, lambda o: across_in(o).wait_recv())
    each(2 - 2 * yh, 4 - 2 * yh, turn_loads)
    each(0, 2, react_other)
    each(1, NGX, lambda r: sum_part(r).start())

    def done_parts(q):
        for c in range(3):
            near_part(q, c).wait_recv()

    opposite_part().wait_recv()
    each(1, 5, done_parts)

    def collect(c):
        total = PO[lax.rem(z + CHUNKS[c], NZ)]
        for q in range(1, 5):
            total = total + RA[q, c].astype(F32)
        return total

    TB[0] = (collect(1) + RA[0, 0].astype(F32)).astype(BF16)
    TB[1] = collect(2).astype(BF16)
    for i in range(2):
        far_part(i).start()
    loads[5].wait()
    each(0, 4, local_forward)

    own_out = pltpu.make_async_copy(OWN, own_h, lsem.at[0])
    own_out.start()

    for s in range(2):
        halo_x(X, HX, 0, s).wait_recv()
        halo_y(X, HY, 1, s).wait_recv()

    def halo_forward(b):
        bx, by = lax.div(b, 2), lax.rem(b, 2)
        m = b * 5 + 1
        fx = link(bx, by, bx) * edge_x(bx)
        fy = link(bx, by, 2 + by) * edge_y(by)
        xs, ys = HX[bx, by], HY[by, bx]
        re = fx * nt(xs, C[m + bx, 0]) + fy * nt(ys, C[m + 2 + by, 0])
        im = fx * nt(xs, C[m + bx, 1]) + fy * nt(ys, C[m + 2 + by, 1])
        RES[bx, by] = RES[bx, by] + re + times_i(im)

    each(0, 4, halo_forward)
    res_out = pltpu.make_async_copy(RES, res_h, lsem.at[1])
    res_out.start()
    for s in range(2):
        halo_x(TX, RX, 2, s).wait_recv()
        halo_y(TY, RY, 3, s).wait_recv()

    def halo_adjoint(b):
        bx, by = lax.div(b, 2), lax.rem(b, 2)
        MULT[bx, by] = MULT[bx, by] + RX[bx, by].astype(F32) + RY[by, bx].astype(F32)

    each(0, 4, halo_adjoint)
    mult_out = pltpu.make_async_copy(MULT, mult_h, lsem.at[2])
    mult_out.start()

    for i in range(2):
        far_gather(i).wait_send()
        swap(i).wait_send()
        halo_x(X, HX, 0, i).wait_send()
        halo_y(X, HY, 1, i).wait_send()
        halo_x(TX, RX, 2, i).wait_send()
        halo_y(TY, RY, 3, i).wait_send()
    opposite_gather().wait_send()
    opposite_part().wait_send()
    each(1, NGX, lambda r: gather(r).wait_send())
    each(0, NZ, lambda o: across(o).wait_send())

    def sent_near(q):
        for c in range(3):
            near_gather(q, c).wait_send()
            near_part(q, c).wait_send()

    each(1, 5, sent_near)

    each(1, NGX, lambda r: sum_part(r).wait_recv())
    total = QB[gx]
    for r in range(1, NGX):
        total = total + RG[r]
    reaction_o[...] = total.astype(BF16)

    kept = collect(0)
    for i in range(2):
        far_part(i).wait_recv()
    pressure_o[...] = kept + RB[0].astype(F32) + RB[1].astype(F32)

    each(1, NGX, lambda r: sum_part(r).wait_send())
    for i in range(2):
        far_part(i).wait_send()
    own_out.wait()
    res_out.wait()
    mult_out.wait()


def finish(lift, scale, pressure, reaction, pmap, res_in, mult_in, own, res_o, mult_o, sens_o):
    b = pl.program_id(0)
    p = pressure[...]
    high = p.astype(BF16)
    low = (p - high.astype(F32)).astype(BF16)
    res_o[...] = res_in[...] + lift * (tn(high, pmap[...]) + tn(low, pmap[...]))
    mult = mult_in[...] + lift * tn(reaction[...], pmap[...])
    mult_o[...] = mult
    sens_o[lax.div(b, 2), lax.rem(b, 2)] = jnp.sum(mult * own[...]) * scale


def on_device(plate_motion, adjoint_load, excitation, coupling, joints, hydro, panel_map):
    lift = math.sqrt(4 * 128 / PD)
    any_ = pl.BlockSpec(memory_space=pl.ANY)
    vm = pl.BlockSpec(memory_space=pltpu.VMEM)
    sm = pl.BlockSpec(memory_space=pltpu.SMEM)
    block = (2, 2, 256, 128)
    panel = (PD, 256)
    dma = pltpu.SemaphoreType.DMA
    whole = jax.ShapeDtypeStruct(block, F32)
    res, mult, own, pressure, reaction, pmap = pl.pallas_call(
        kernel,
        out_shape=(
            whole, whole, whole,
            jax.ShapeDtypeStruct(panel, F32),
            jax.ShapeDtypeStruct(panel, BF16),
            jax.ShapeDtypeStruct((PD, 512), BF16),
        ),
        in_specs=[sm, any_, any_, any_, any_, any_, any_],
        out_specs=(any_, any_, any_, vm, vm, vm),
        scratch_shapes=[
            pltpu.VMEM(block, BF16),
            pltpu.VMEM(block, BF16),
            pltpu.VMEM(block, BF16),
            pltpu.VMEM(block, BF16),
            pltpu.VMEM((20, 2, 128, 128), BF16),
            pltpu.VMEM((2, 1024, 512), BF16),
            pltpu.VMEM((2, 4, 512, 256), BF16),
            pltpu.VMEM((128, 128), BF16),
            pltpu.VMEM((128, 128), F32),
            pltpu.VMEM((NGX,) + panel, BF16),
            pltpu.VMEM((NGX * PD, 256), BF16),
            pltpu.VMEM((NGY,) + panel, BF16),
            pltpu.VMEM((4, 256, 256), BF16),
            pltpu.VMEM((NZ,) + panel, F32),
            pltpu.VMEM((NZ,) + panel, BF16),
            pltpu.VMEM((NZ,) + panel, BF16),
            pltpu.VMEM((NZ,) + panel, BF16),
            pltpu.VMEM((5, 3) + panel, BF16),
            pltpu.VMEM((2,) + panel, BF16),
            pltpu.VMEM((2,) + panel, BF16),
            pltpu.VMEM((NGX,) + panel, F32),
            pltpu.VMEM((NGX,) + panel, F32),
            pltpu.VMEM(block, BF16),
            pltpu.VMEM(block, BF16),
            pltpu.VMEM(block, BF16),
            pltpu.VMEM(block, BF16),
            pltpu.VMEM(block, BF16),
            pltpu.VMEM(block, BF16),
            pltpu.VMEM(block, F32),
            pltpu.VMEM(block, F32),
            pltpu.VMEM(block, F32),
            dma((6,)),
            dma((NGX,)), dma((NGX,)),
            dma((2,)), dma((2,)),
            dma((5, 3)), dma((5, 3)),
            dma((NZ,)), dma((NZ,)),
            dma((2,)), dma((2,)),
            dma((5, 3)), dma((5, 3)),
            dma((2,)), dma((2,)),
            dma((NGX,)), dma((NGX,)),
            dma((4, 2)), dma((4, 2)),
        ],
        compiler_params=pltpu.CompilerParams(
            collective_id=0, has_side_effects=True, vmem_limit_bytes=62 << 20),
        name="plate",
    )(
        joints,
        plate_motion.reshape(block),
        adjoint_load.reshape(block),
        excitation.reshape(block),
        coupling.reshape(20, 2, 128, 128),
        hydro,
        panel_map.reshape(128, 128),
    )
    tile = pl.BlockSpec((None, None, 256, 128), lambda b: (b // 2, b % 2, 0, 0))
    fixed = pl.BlockSpec(panel, lambda b: (0, 0))
    res, mult, sens = pl.pallas_call(
        functools.partial(finish, lift, 1.0 / 128.0),
        grid=(4,),
        out_shape=(whole, whole, jax.ShapeDtypeStruct((2, 2), F32)),
        in_specs=[fixed, fixed, pl.BlockSpec((PD, 128), lambda b: (0, b)), tile, tile, tile],
        out_specs=(tile, tile, sm),
        compiler_params=pltpu.CompilerParams(vmem_limit_bytes=62 << 20),
        name="finish",
    )(pressure, reaction, pmap, res, mult, own)
    shape = plate_motion.shape
    return res.reshape(shape), mult.reshape(shape), sens


def solution(mesh):
    placed = (
        P("gx", "gy", None, None, None),
        P("gx", "gy", None, None, None),
        P("gx", "gy", None, None, None),
        P("gx", "gy", None, None, None, None),
        P("gx", "gy", None),
        P(None, "gx", "gy"),
        P(("gx", "gy"), None, None, None),
    )
    return jax.shard_map(
        on_device,
        mesh=mesh,
        in_specs=placed,
        out_specs=(P("gx", "gy", None, None, None), P("gx", "gy", None, None, None), P("gx", "gy")),
        check_vma=False,
    )
```

```python
import functools
import math

import jax
import jax.numpy as jnp
from jax import lax
from jax.experimental import pallas as pl
from jax.experimental.pallas import tpu as pltpu
from jax.sharding import PartitionSpec as P

MESH = pl.DeviceIdType.MESH
F32 = jnp.float32
BF16 = jnp.bfloat16
NGX, NGY, NZ = 16, 32, 16
PD = 32
FAR = 5
CHUNKS = (0, FAR, NZ - FAR)


def nn(a, b):
    return jnp.dot(a, b, preferred_element_type=F32)


def nt(a, b):
    return lax.dot_general(a, b, (((1,), (1,)), ((), ())), preferred_element_type=F32)


def tn(a, b):
    return lax.dot_general(a, b, (((0,), (0,)), ((), ())), preferred_element_type=F32)


def times_i(x):
    rows = x.shape[0]
    even = lax.rem(lax.broadcasted_iota(jnp.int32, x.shape, 0), 2) == 0
    return jnp.where(even, -pltpu.roll(x, rows - 1, 0), pltpu.roll(x, 1, 0))


def lane_i(width):
    r = lax.broadcasted_iota(jnp.int32, (width, width), 0)
    c = lax.broadcasted_iota(jnp.int32, (width, width), 1)
    odd = lax.rem(c, 2) == 1
    plus = jnp.where(jnp.logical_and(odd, r == c - 1), 1.0, 0.0)
    minus = jnp.where(jnp.logical_and(jnp.logical_not(odd), r == c + 1), 1.0, 0.0)
    return (plus - minus).astype(BF16)


def kernel(
    joints_h, plate_h, adj_h, exc_h, coup_h, hyd_h, pmap_h,
    RES, MULT, OWN, pressure_o, reaction_o, map_o,
    X, A, JA, E, C, H, HT, PM, PM32, MG, MP, LG, LP, PB, RA, T, TB, RB, QB, RG,
    HX, HY, TX, TY, RX, RY, joints,
    lsem, gx_s, gx_r, fa_s, fa_r, nb_s, nb_r, yf_s, yf_r,
    ra_s, ra_r, rb_s, rb_r, rx_s, rx_r, h_s, h_r,
):
    gx = lax.axis_index("gx")
    gy = lax.axis_index("gy")
    yh = lax.div(gy, NZ)
    z = lax.rem(gy, NZ)

    def gx_at(r):
        return lax.rem(gx + r, NGX)

    def gy_at(dz, dy):
        return lax.rem(yh + dy, 2) * NZ + lax.rem(z + dz, NZ)

    def near(q):
        return lax.rem(lax.rem(q + 2, 5) - 2 + NZ, NZ)

    def each(lo, hi, f):
        def body(i, carry):
            f(i)
            return carry
        lax.fori_loop(lo, hi, body, 0)

    def remote(src, dst, send, recv, where):
        return pltpu.make_async_remote_copy(
            src, dst, send, recv, device_id=where, device_id_type=MESH)

    loads = [
        pltpu.make_async_copy(s, d, lsem.at[i])
        for i, (s, d) in enumerate(
            ((pmap_h, PM), (adj_h, A), (plate_h, X), (coup_h, C), (hyd_h, H), (exc_h, E),
             (joints_h, joints))
        )
    ]
    for c in loads:
        c.start()

    bar = pltpu.get_barrier_semaphore()

    def greet(x, y):
        pl.semaphore_signal(bar, inc=1, device_id=(x, y), device_id_type=MESH)

    for dz in (FAR, NZ - FAR, 3, NZ - 3):
        greet(gx, gy_at(dz, 0))
    greet(gx, gy_at(0, 1))
    for step in (1, NGY - 1):
        greet(gx, lax.rem(gy + step, NGY))
    each(1, 5, lambda q: greet(gx, gy_at(near(q), 0)))
    each(1, NGX, lambda r: greet(gx_at(r), gy))

    def far_gather(i):
        return remote(LG.at[gy], LG.at[gy], fa_s.at[i], fa_r.at[i],
                      (gx, gy_at((FAR, NZ - FAR)[i], 0)))

    def far_gather_in(i):
        slot = gy_at((NZ - FAR, FAR)[i], 0)
        return remote(LG.at[slot], LG.at[slot], fa_s.at[i], fa_r.at[i], (gx, slot))

    def gather(r):
        return remote(MG.at[gx], MG.at[gx], gx_s.at[r], gx_r.at[r], (gx_at(r), gy))

    def gather_in(r):
        slot = gx_at(NGX - r)
        return remote(MG.at[slot], MG.at[slot], gx_s.at[r], gx_r.at[r], (slot, gy))

    def near_gather(q, c):
        slot = gy_at(CHUNKS[c], 0)
        return remote(LG.at[slot], LG.at[slot], nb_s.at[q, c], nb_r.at[q, c],
                      (gx, gy_at(near(q), 0)))

    def near_slot(q, c):
        return lax.rem(NZ - near(q) + CHUNKS[c], NZ)

    def near_gather_in(q, c):
        slot = gy_at(near_slot(q, c), 0)
        return remote(LG.at[slot], LG.at[slot], nb_s.at[q, c], nb_r.at[q, c], (gx, slot))

    def opposite_gather():
        slot = gy_at(NZ - FAR, 0)
        return remote(LG.at[slot], LG.at[slot], nb_s.at[0, 0], nb_r.at[0, 0], (gx, gy_at(3, 0)))

    def opposite_gather_in():
        slot = gy_at(8, 0)
        return remote(LG.at[slot], LG.at[slot], nb_s.at[0, 0], nb_r.at[0, 0], (gx, slot))

    def across(o):
        slot = gy_at(o, 0)
        return remote(LG.at[slot], LG.at[slot], yf_s.at[o], yf_r.at[o], (gx, gy_at(0, 1)))

    def across_in(o):
        slot = gy_at(o, 1)
        return remote(LG.at[slot], LG.at[slot], yf_s.at[o], yf_r.at[o], (gx, gy_at(0, 1)))

    def near_part(q, c):
        return remote(PB.at[:, lax.rem(z + near(q) + CHUNKS[c], NZ)], RA.at[q, c],
                      ra_s.at[q, c], ra_r.at[q, c], (gx, gy_at(near(q), 0)))

    def opposite_part():
        return remote(PB.at[:, lax.rem(z + 8, NZ)], RA.at[0, 0],
                      ra_s.at[0, 0], ra_r.at[0, 0], (gx, gy_at(3, 0)))

    def far_part(i):
        dz, dy = ((0, 1), (FAR, 0), (NZ - FAR, 0), (FAR, 1), (NZ - FAR, 1))[i]
        return remote(TB.at[i], RB.at[i], rb_s.at[i], rb_r.at[i], (gx, gy_at(dz, dy)))

    def sum_part(r):
        return remote(QB.at[gx_at(r)], RG.at[r], rx_s.at[r], rx_r.at[r], (gx_at(r), gy))

    def side(gap, s):
        return gap if s else -gap

    def halo_x(src, dst, k, s):
        return remote(src.at[s], dst.at[1 - s], h_s.at[k, s], h_r.at[k, 1 - s],
                      (gx + side(1, s), gy))

    def halo_x_in(src, dst, k, s):
        return remote(src.at[s], dst.at[s], h_s.at[k, s], h_r.at[k, s], (gx + side(1, s), gy))

    def halo_y(src, dst, k, s):
        return remote(src.at[:, s] if k == 1 else src.at[s], dst.at[1 - s],
                      h_s.at[k, s], h_r.at[k, 1 - s], (gx, gy + side(1, s)))

    def halo_y_in(src, dst, k, s):
        return remote(src.at[:, s] if k == 1 else src.at[s], dst.at[s],
                      h_s.at[k, s], h_r.at[k, s], (gx, gy + side(1, s)))

    loads[0].wait()
    PM32[...] = PM[...].astype(F32)
    for b in range(4):
        map_o[:, b * 128:(b + 1) * 128] = PM32[pl.ds(b, PD, stride=4), :].astype(BF16)

    def panels(V):
        total = nt(map_o[:, 0:128], V[0, 0])
        for b in range(1, 4):
            total = total + nt(map_o[:, b * 128:(b + 1) * 128], V[b // 2, b % 2])
        return total.astype(BF16)

    loads[1].wait()
    LG[gy] = panels(A)
    loads[2].wait()
    MG[gx] = panels(X)

    loads[3].wait()
    loads[6].wait()

    def link(bx, by, d):
        return joints[bx, by, d].astype(F32)

    def edge_x(bx):
        v = gx + 2 * bx - 1
        return jnp.where(jnp.logical_and(v >= 0, v < NGX), 1.0, 0.0).astype(F32)

    def edge_y(by):
        v = gy + 2 * by - 1
        return jnp.where(jnp.logical_and(v >= 0, v < NGY), 1.0, 0.0).astype(F32)

    def back(bx, by, d):
        m = (bx * 2 + by) * 5 + d
        return nn(A[bx, by], C[m, 0]) - nn(JA[bx, by], C[m, 1])

    def outgoing(b):
        bx, by = lax.div(b, 2), lax.rem(b, 2)
        JA[bx, by] = times_i(A[bx, by].astype(F32)).astype(BF16)
        TX[bx, by] = (link(bx, by, bx) * edge_x(bx) * back(bx, by, 1 + bx)).astype(BF16)
        TY[by, bx] = (link(bx, by, 2 + by) * edge_y(by) * back(bx, by, 3 + by)).astype(BF16)

    each(0, 4, outgoing)
    def to_x(s):
        return gx + 1 < NGX if s else gx > 0

    def to_y(s):
        return gy + 1 < NGY if s else gy > 0

    def sent_halos(s):
        @pl.when(to_x(s))
        def _():
            halo_x(X, HX, 0, s).wait_send()
            halo_x(TX, RX, 2, s).wait_send()

        @pl.when(to_y(s))
        def _():
            halo_y(X, HY, 1, s).wait_send()
            halo_y(TY, RY, 3, s).wait_send()

    def crosses(s):
        return z == NZ - 1 if s else z == 0

    def start_crossing():
        for s in range(2):
            @pl.when(jnp.logical_and(to_y(s), crosses(s)))
            def _():
                halo_y(X, HY, 1, s).start()
                halo_y(TY, RY, 3, s).start()

    def start_halos(k):
        for s in range(2):
            @pl.when(to_x(s))
            def _():
                halo_x(*((X, HX), (TX, RX))[k], 2 * k, s).start()

            @pl.when(jnp.logical_and(to_y(s), jnp.logical_not(crosses(s))))
            def _():
                halo_y(*((X, HY), (TY, RY))[k], 2 * k + 1, s).start()

    def wait_halos(k):
        for s in range(2):
            @pl.when(to_x(s))
            def _():
                src, dst = ((X, HX), (TX, RX))[k]
                halo_x_in(src, dst, 2 * k, s).wait_recv()

            @pl.when(to_y(s))
            def _():
                src, dst = ((X, HY), (TY, RY))[k]
                halo_y_in(src, dst, 2 * k + 1, s).wait_recv()

    pl.semaphore_wait(bar, 4 + 1 + 2 + 4 + 15)

    for i in range(2):
        far_gather(i).start()
    each(1, NGX, lambda r: gather(r).start())
    across(0).start()
    start_crossing()
    start_halos(0)
    each(1, 5, lambda q: near_gather(q, 0).start())

    loads[4].wait()
    jm = lane_i(256)

    def turn(t):
        rows = pl.ds(pl.multiple_of(t * 256, 256), 256)
        for c in range(2):
            HT[c, t] = H[c, rows, :].T

    each(0, 2, turn)

    def pass_on(c):
        def go(q):
            near_gather_in(q, c).wait_recv()
            across(near_slot(q, c)).start()
        each(1, 5, go)

    far_gather_in(0).wait_recv()
    opposite_gather().start()
    each(1, 5, lambda q: near_gather(q, 2).start())
    far_gather_in(1).wait_recv()
    each(1, 5, lambda q: near_gather(q, 1).start())

    each(1, NGX, lambda r: gather_in(r).wait_recv())
    MP[...] = nn(MG[...].reshape(NGX * PD, 256), jm).astype(BF16)

    def press(t):
        rows = pl.ds(pl.multiple_of(t * 256, 256), 256)
        p = nn(H[0, rows, :], MG[...].reshape(NGX * PD, 256)) + nn(H[1, rows, :], MP[...])
        PB[lax.div(t, 2), pl.ds(lax.rem(t, 2) * 8, 8)] = p.astype(BF16).reshape(8, PD, 256)

    each(0, 4, press)

    def start_parts(q):
        for c in (1, 2, 0):
            near_part(q, c).start()

    opposite_part().start()
    each(1, 5, start_parts)
    across(NZ - FAR).start()
    across(FAR).start()
    pass_on(0)

    each(2, 4, turn)

    def local_forward(b):
        bx, by = lax.div(b, 2), lax.rem(b, 2)
        m = b * 5
        x = X[bx, by]
        own = nt(x, C[m, 0]) + times_i(nt(x, C[m, 1]))
        OWN[bx, by] = own
        dx, dy = 1 - bx, 3 - by
        fx, fy = link(bx, by, dx), link(bx, by, dy)
        xs, ys = X[1 - bx, by], X[bx, 1 - by]
        re = fx * nt(xs, C[m + 1 + dx, 0]) + fy * nt(ys, C[m + 1 + dy, 0])
        im = fx * nt(xs, C[m + 1 + dx, 1]) + fy * nt(ys, C[m + 1 + dy, 1])
        RES[bx, by] = own + re + times_i(im) - E[bx, by].astype(F32)

    def local_adjoint(b):
        bx, by = lax.div(b, 2), lax.rem(b, 2)
        MULT[bx, by] = (
            back(bx, by, 0)
            + link(1 - bx, by, bx) * back(1 - bx, by, 1 + bx)
            + link(bx, 1 - by, 2 + by) * back(bx, 1 - by, 3 + by))

    each(0, 4, local_adjoint)

    opposite_gather_in().wait_recv()
    across(8).start()

    pass_on(2)
    pass_on(1)
    start_halos(1)

    def turn_loads(k):
        LP[k] = nn(LG[pl.ds(k * 8, 8)].reshape(256, 256), jm).astype(BF16)

    def react(y, t):
        rows = pl.ds(pl.multiple_of(t * 256, 256), 256)
        total = jnp.zeros((256, 256), F32)
        for i in range(2):
            k = 2 * y + i
            total = total + nn(HT[0, k, rows, :], LG[pl.ds(k * 8, 8)].reshape(256, 256))
            total = total - nn(HT[1, k, rows, :], LP[k])
        return total.reshape(8, PD, 256)

    def react_own(t):
        QB[pl.ds(t * 8, 8)] = react(yh, t)

    def react_other(t):
        rows = pl.ds(t * 8, 8)
        QB[rows] = QB[rows] + react(1 - yh, t)

    each(2 * yh, 2 * yh + 2, turn_loads)
    each(0, 2, react_own)
    each(0, NZ, lambda o: across_in(o).wait_recv())
    each(2 - 2 * yh, 4 - 2 * yh, turn_loads)
    each(0, 2, react_other)
    each(1, NGX, lambda r: sum_part(r).start())

    def done_parts(q):
        for c in range(3):
            near_part(q, c).wait_recv()

    opposite_part().wait_recv()
    each(1, 5, done_parts)

    for c in range(3):
        total = PB[:, lax.rem(z + CHUNKS[c], NZ)].astype(F32)
        for q in range(0 if c == 1 else 1, 5):
            total = total + RA[q, c if q else 0].astype(F32)
        T[c] = total
    for i, (c, dy) in enumerate(((0, 1), (1, 0), (2, 0), (1, 1), (2, 1))):
        TB[i] = T[c, lax.rem(yh + dy, 2)].astype(BF16)
    for i in (4, 3, 2, 1, 0):
        far_part(i).start()
    loads[5].wait()
    each(0, 4, local_forward)

    wait_halos(0)

    def halo_forward(b):
        bx, by = lax.div(b, 2), lax.rem(b, 2)
        m = b * 5 + 1
        fx = link(bx, by, bx) * edge_x(bx)
        fy = link(bx, by, 2 + by) * edge_y(by)
        xs = jnp.where(edge_x(bx) > 0.5, HX[bx, by], jnp.zeros((256, 128), BF16))
        ys = jnp.where(edge_y(by) > 0.5, HY[by, bx], jnp.zeros((256, 128), BF16))
        re = fx * nt(xs, C[m + bx, 0]) + fy * nt(ys, C[m + 2 + by, 0])
        im = fx * nt(xs, C[m + bx, 1]) + fy * nt(ys, C[m + 2 + by, 1])
        RES[bx, by] = RES[bx, by] + re + times_i(im)

    each(0, 4, halo_forward)
    wait_halos(1)

    def halo_adjoint(b):
        bx, by = lax.div(b, 2), lax.rem(b, 2)
        xs = jnp.where(edge_x(bx) > 0.5, RX[bx, by].astype(F32), 0.0)
        ys = jnp.where(edge_y(by) > 0.5, RY[by, bx].astype(F32), 0.0)
        MULT[bx, by] = MULT[bx, by] + xs + ys

    each(0, 4, halo_adjoint)

    for i in range(2):
        far_gather(i).wait_send()
        sent_halos(i)
    opposite_gather().wait_send()
    opposite_part().wait_send()
    each(1, NGX, lambda r: gather(r).wait_send())
    each(0, NZ, lambda o: across(o).wait_send())

    def sent_near(q):
        for c in range(3):
            near_gather(q, c).wait_send()
            near_part(q, c).wait_send()

    each(1, 5, sent_near)

    each(1, NGX, lambda r: sum_part(r).wait_recv())
    total = QB[gx]
    for r in range(1, NGX):
        total = total + RG[r]
    reaction_o[...] = total.astype(BF16)

    total = T[0, yh]
    for i in range(5):
        far_part(i).wait_recv()
        total = total + RB[i].astype(F32)
    pressure_o[...] = total

    each(1, NGX, lambda r: sum_part(r).wait_send())
    for i in range(5):
        far_part(i).wait_send()


def finish(lift, scale, pressure, reaction, pmap, res_in, mult_in, own, res_h, mult_h, sens_o,
           res_v, mult_v, sem):
    p = pressure[...]
    high = p.astype(BF16)
    low = (p - high.astype(F32)).astype(BF16)
    copies = []
    for b in range(4):
        at = (b // 2, b % 2)
        m = pmap[:, b * 128:(b + 1) * 128]
        mult = mult_in[at] + lift * tn(reaction[...], m)
        mult_v[at] = mult
        copies.append(pltpu.make_async_copy(mult_v.at[at], mult_h.at[at], sem.at[0, b]))
        copies[-1].start()
        res_v[at] = res_in[at] + lift * (tn(high, m) + tn(low, m))
        copies.append(pltpu.make_async_copy(res_v.at[at], res_h.at[at], sem.at[1, b]))
        copies[-1].start()
        sens_o[at] = jnp.sum(mult * own[at]) * scale
    for c in copies:
        c.wait()


def on_device(plate_motion, adjoint_load, excitation, coupling, joints, hydro, panel_map):
    lift = math.sqrt(4 * 128 / PD)
    hbm = pl.BlockSpec(memory_space=pltpu.HBM)
    vm = pl.BlockSpec(memory_space=pltpu.VMEM)
    sm = pl.BlockSpec(memory_space=pltpu.SMEM)
    block = (2, 2, 256, 128)
    panel = (PD, 256)
    dma = pltpu.SemaphoreType.DMA
    whole = jax.ShapeDtypeStruct(block, F32)
    res, mult, own, pressure, reaction, pmap = pl.pallas_call(
        kernel,
        out_shape=(
            whole, whole, whole,
            jax.ShapeDtypeStruct(panel, F32),
            jax.ShapeDtypeStruct(panel, BF16),
            jax.ShapeDtypeStruct((PD, 512), BF16),
        ),
        in_specs=[hbm] * 7,
        out_specs=(vm,) * 6,
        scratch_shapes=[
            pltpu.VMEM(block, BF16),
            pltpu.VMEM(block, BF16),
            pltpu.VMEM(block, BF16),
            pltpu.VMEM(block, BF16),
            pltpu.VMEM((20, 2, 128, 128), BF16),
            pltpu.VMEM((2, 1024, 512), BF16),
            pltpu.VMEM((2, 4, 512, 256), BF16),
            pltpu.VMEM((128, 128), BF16),
            pltpu.VMEM((128, 128), F32),
            pltpu.VMEM((NGX,) + panel, BF16),
            pltpu.VMEM((NGX * PD, 256), BF16),
            pltpu.VMEM((NGY,) + panel, BF16),
            pltpu.VMEM((4, 256, 256), BF16),
            pltpu.VMEM((2, NZ) + panel, BF16),
            pltpu.VMEM((5, 3, 2) + panel, BF16),
            pltpu.VMEM((3, 2) + panel, F32),
            pltpu.VMEM((5,) + panel, BF16),
            pltpu.VMEM((5,) + panel, BF16),
            pltpu.VMEM((NGX,) + panel, F32),
            pltpu.VMEM((NGX,) + panel, F32),
            pltpu.VMEM(block, BF16),
            pltpu.VMEM(block, BF16),
            pltpu.VMEM(block, BF16),
            pltpu.VMEM(block, BF16),
            pltpu.VMEM(block, BF16),
            pltpu.VMEM(block, BF16),
            pltpu.SMEM((2, 2, 4), jnp.int32),
            dma((7,)),
            dma((NGX,)), dma((NGX,)),
            dma((2,)), dma((2,)),
            dma((5, 3)), dma((5, 3)),
            dma((NZ,)), dma((NZ,)),
            dma((5, 3)), dma((5, 3)),
            dma((5,)), dma((5,)),
            dma((NGX,)), dma((NGX,)),
            dma((4, 2)), dma((4, 2)),
        ],
        compiler_params=pltpu.CompilerParams(
            collective_id=0, has_side_effects=True, vmem_limit_bytes=32 << 20),
        name="plate",
    )(
        *(pltpu.with_memory_space_constraint(x, pltpu.HBM) for x in (
            joints,
            plate_motion.reshape(block),
            adjoint_load.reshape(block),
            excitation.reshape(block),
            coupling.reshape(20, 2, 128, 128),
            hydro,
            panel_map.reshape(128, 128))),
    )
    res, mult, sens = pl.pallas_call(
        functools.partial(finish, lift, 1.0 / 128.0),
        out_shape=(whole, whole, jax.ShapeDtypeStruct((2, 2), F32)),
        in_specs=[vm] * 6,
        out_specs=(hbm, hbm, sm),
        scratch_shapes=[pltpu.VMEM(block, F32)] * 2 + [dma((2, 4))],
        compiler_params=pltpu.CompilerParams(vmem_limit_bytes=32 << 20),
        name="finish",
    )(pressure, reaction, pmap, res, mult, own)
    shape = plate_motion.shape
    return res.reshape(shape), mult.reshape(shape), sens


def solution(mesh):
    placed = (
        P("gx", "gy", None, None, None),
        P("gx", "gy", None, None, None),
        P("gx", "gy", None, None, None),
        P("gx", "gy", None, None, None, None),
        P("gx", "gy", None),
        P(None, "gx", "gy"),
        P(("gx", "gy"), None, None, None),
    )
    return jax.shard_map(
        on_device,
        mesh=mesh,
        in_specs=placed,
        out_specs=(P("gx", "gy", None, None, None), P("gx", "gy", None, None, None), P("gx", "gy")),
        check_vma=False,
    )
```

```python
import functools
import math

import jax
import jax.numpy as jnp
from jax import lax
from jax.experimental import pallas as pl
from jax.experimental.pallas import tpu as pltpu
from jax.sharding import PartitionSpec as P

MESH = pl.DeviceIdType.MESH
F32 = jnp.float32
BF16 = jnp.bfloat16
NGX, NGY, NZ = 16, 32, 16
PD = 32
FAR = 5
CHUNKS = (0, FAR, NZ - FAR)


def nn(a, b):
    return jnp.dot(a, b, preferred_element_type=F32)


def nt(a, b):
    return lax.dot_general(a, b, (((1,), (1,)), ((), ())), preferred_element_type=F32)


def tn(a, b):
    return lax.dot_general(a, b, (((0,), (0,)), ((), ())), preferred_element_type=F32)


def times_i(x):
    rows = x.shape[0]
    even = lax.rem(lax.broadcasted_iota(jnp.int32, x.shape, 0), 2) == 0
    return jnp.where(even, -pltpu.roll(x, rows - 1, 0), pltpu.roll(x, 1, 0))


def lane_i(width):
    r = lax.broadcasted_iota(jnp.int32, (width, width), 0)
    c = lax.broadcasted_iota(jnp.int32, (width, width), 1)
    odd = lax.rem(c, 2) == 1
    plus = jnp.where(jnp.logical_and(odd, r == c - 1), 1.0, 0.0)
    minus = jnp.where(jnp.logical_and(jnp.logical_not(odd), r == c + 1), 1.0, 0.0)
    return (plus - minus).astype(BF16)


def kernel(
    joints_h, plate_h, adj_h, exc_h, coup_h, hyd_h, pmap_h,
    RES, MULT, OWN, pressure_o, reaction_o, map_o,
    X, A, JA, E, C, H, HT, PM, PM32, MG, MP, LG, LP, PB, RA, T, TB, RB, QB, RG,
    HX, HY, TX, TY, RX, RY, joints,
    lsem, gx_s, gx_r, fa_s, fa_r, nb_s, nb_r, yf_s, yf_r,
    ra_s, ra_r, rb_s, rb_r, rx_s, rx_r, h_s, h_r,
):
    gx = lax.axis_index("gx")
    gy = lax.axis_index("gy")
    yh = lax.div(gy, NZ)
    z = lax.rem(gy, NZ)

    def gx_at(r):
        return lax.rem(gx + r, NGX)

    def gy_at(dz, dy):
        return lax.rem(yh + dy, 2) * NZ + lax.rem(z + dz, NZ)

    def near(q):
        return lax.rem(lax.rem(q + 2, 5) - 2 + NZ, NZ)

    def each(lo, hi, f):
        def body(i, carry):
            f(i)
            return carry
        lax.fori_loop(lo, hi, body, 0)

    def remote(src, dst, send, recv, where):
        return pltpu.make_async_remote_copy(
            src, dst, send, recv, device_id=where, device_id_type=MESH)

    loads = [
        pltpu.make_async_copy(s, d, lsem.at[i])
        for i, (s, d) in enumerate(
            ((pmap_h, PM), (adj_h, A), (plate_h, X), (coup_h, C), (hyd_h, H), (exc_h, E),
             (joints_h, joints))
        )
    ]
    for c in loads:
        c.start()

    bar = pltpu.get_barrier_semaphore()

    def greet(x, y):
        pl.semaphore_signal(bar, inc=1, device_id=(x, y), device_id_type=MESH)

    for dz in (FAR, NZ - FAR, 3, NZ - 3):
        greet(gx, gy_at(dz, 0))
    greet(gx, gy_at(0, 1))
    for step in (1, NGY - 1):
        greet(gx, lax.rem(gy + step, NGY))
    each(1, 5, lambda q: greet(gx, gy_at(near(q), 0)))
    each(1, NGX, lambda r: greet(gx_at(r), gy))

    def far_gather(i):
        return remote(LG.at[gy], LG.at[gy], fa_s.at[i], fa_r.at[i],
                      (gx, gy_at((FAR, NZ - FAR)[i], 0)))

    def far_gather_in(i):
        slot = gy_at((NZ - FAR, FAR)[i], 0)
        return remote(LG.at[slot], LG.at[slot], fa_s.at[i], fa_r.at[i], (gx, slot))

    def gather(r):
        return remote(MG.at[gx], MG.at[gx], gx_s.at[r], gx_r.at[r], (gx_at(r), gy))

    def gather_in(r):
        slot = gx_at(NGX - r)
        return remote(MG.at[slot], MG.at[slot], gx_s.at[r], gx_r.at[r], (slot, gy))

    def near_gather(q, c):
        slot = gy_at(CHUNKS[c], 0)
        return remote(LG.at[slot], LG.at[slot], nb_s.at[q, c], nb_r.at[q, c],
                      (gx, gy_at(near(q), 0)))

    def near_slot(q, c):
        return lax.rem(NZ - near(q) + CHUNKS[c], NZ)

    def near_gather_in(q, c):
        slot = gy_at(near_slot(q, c), 0)
        return remote(LG.at[slot], LG.at[slot], nb_s.at[q, c], nb_r.at[q, c], (gx, slot))

    def opposite_gather():
        slot = gy_at(NZ - FAR, 0)
        return remote(LG.at[slot], LG.at[slot], nb_s.at[0, 0], nb_r.at[0, 0], (gx, gy_at(3, 0)))

    def opposite_gather_in():
        slot = gy_at(8, 0)
        return remote(LG.at[slot], LG.at[slot], nb_s.at[0, 0], nb_r.at[0, 0], (gx, slot))

    def across(o):
        slot = gy_at(o, 0)
        return remote(LG.at[slot], LG.at[slot], yf_s.at[o], yf_r.at[o], (gx, gy_at(0, 1)))

    def across_in(o):
        slot = gy_at(o, 1)
        return remote(LG.at[slot], LG.at[slot], yf_s.at[o], yf_r.at[o], (gx, gy_at(0, 1)))

    def near_part(q, c):
        return remote(PB.at[:, lax.rem(z + near(q) + CHUNKS[c], NZ)], RA.at[q, c],
                      ra_s.at[q, c], ra_r.at[q, c], (gx, gy_at(near(q), 0)))

    def opposite_part():
        return remote(PB.at[:, lax.rem(z + 8, NZ)], RA.at[0, 0],
                      ra_s.at[0, 0], ra_r.at[0, 0], (gx, gy_at(3, 0)))

    def far_part(i):
        dz, dy = ((0, 1), (FAR, 0), (NZ - FAR, 0), (FAR, 1), (NZ - FAR, 1))[i]
        return remote(TB.at[i], RB.at[i], rb_s.at[i], rb_r.at[i], (gx, gy_at(dz, dy)))

    def sum_part(r):
        return remote(QB.at[gx_at(r)], RG.at[r], rx_s.at[r], rx_r.at[r], (gx_at(r), gy))

    def side(gap, s):
        return gap if s else -gap

    def halo_x(src, dst, k, s):
        return remote(src.at[s], dst.at[1 - s], h_s.at[k, s], h_r.at[k, 1 - s],
                      (gx + side(1, s), gy))

    def halo_x_in(src, dst, k, s):
        return remote(src.at[s], dst.at[s], h_s.at[k, s], h_r.at[k, s], (gx + side(1, s), gy))

    def halo_y(src, dst, k, s):
        return remote(src.at[:, s] if k == 1 else src.at[s], dst.at[1 - s],
                      h_s.at[k, s], h_r.at[k, 1 - s], (gx, gy + side(1, s)))

    def halo_y_in(src, dst, k, s):
        return remote(src.at[:, s] if k == 1 else src.at[s], dst.at[s],
                      h_s.at[k, s], h_r.at[k, s], (gx, gy + side(1, s)))

    loads[0].wait()
    PM32[...] = PM[...].astype(F32)
    for b in range(4):
        map_o[:, b * 128:(b + 1) * 128] = PM32[pl.ds(b, PD, stride=4), :].astype(BF16)

    def panels(V):
        total = nt(map_o[:, 0:128], V[0, 0])
        for b in range(1, 4):
            total = total + nt(map_o[:, b * 128:(b + 1) * 128], V[b // 2, b % 2])
        return total.astype(BF16)

    loads[1].wait()
    LG[gy] = panels(A)
    loads[2].wait()
    MG[gx] = panels(X)

    loads[3].wait()
    loads[6].wait()

    def link(bx, by, d):
        return joints[bx, by, d].astype(F32)

    def edge_x(bx):
        v = gx + 2 * bx - 1
        return jnp.where(jnp.logical_and(v >= 0, v < NGX), 1.0, 0.0).astype(F32)

    def edge_y(by):
        v = gy + 2 * by - 1
        return jnp.where(jnp.logical_and(v >= 0, v < NGY), 1.0, 0.0).astype(F32)

    def back(bx, by, d):
        m = (bx * 2 + by) * 5 + d
        return nn(A[bx, by], C[m, 0]) - nn(JA[bx, by], C[m, 1])

    def outgoing(b):
        bx, by = lax.div(b, 2), lax.rem(b, 2)
        JA[bx, by] = times_i(A[bx, by].astype(F32)).astype(BF16)
        TX[bx, by] = (link(bx, by, bx) * edge_x(bx) * back(bx, by, 1 + bx)).astype(BF16)
        TY[by, bx] = (link(bx, by, 2 + by) * edge_y(by) * back(bx, by, 3 + by)).astype(BF16)

    each(0, 4, outgoing)
    def to_x(s):
        return gx + 1 < NGX if s else gx > 0

    def to_y(s):
        return gy + 1 < NGY if s else gy > 0

    def sent_halos(s):
        @pl.when(to_x(s))
        def _():
            halo_x(X, HX, 0, s).wait_send()
            halo_x(TX, RX, 2, s).wait_send()

        @pl.when(to_y(s))
        def _():
            halo_y(X, HY, 1, s).wait_send()
            halo_y(TY, RY, 3, s).wait_send()

    def crosses(s):
        return z == NZ - 1 if s else z == 0

    def start_crossing():
        for s in range(2):
            @pl.when(jnp.logical_and(to_y(s), crosses(s)))
            def _():
                halo_y(X, HY, 1, s).start()
                halo_y(TY, RY, 3, s).start()

    def start_halos(k):
        for s in range(2):
            @pl.when(to_x(s))
            def _():
                halo_x(*((X, HX), (TX, RX))[k], 2 * k, s).start()

            @pl.when(jnp.logical_and(to_y(s), jnp.logical_not(crosses(s))))
            def _():
                halo_y(*((X, HY), (TY, RY))[k], 2 * k + 1, s).start()

    def wait_halos(k):
        for s in range(2):
            @pl.when(to_x(s))
            def _():
                src, dst = ((X, HX), (TX, RX))[k]
                halo_x_in(src, dst, 2 * k, s).wait_recv()

            @pl.when(to_y(s))
            def _():
                src, dst = ((X, HY), (TY, RY))[k]
                halo_y_in(src, dst, 2 * k + 1, s).wait_recv()

    pl.semaphore_wait(bar, 4 + 1 + 2 + 4 + 15)

    for i in range(2):
        far_gather(i).start()
    each(1, NGX, lambda r: gather(r).start())
    across(0).start()
    start_halos(0)
    each(1, 5, lambda q: near_gather(q, 0).start())

    loads[4].wait()
    jm = lane_i(256)

    def turn(t):
        rows = pl.ds(pl.multiple_of(t * 256, 256), 256)
        for c in range(2):
            HT[c, t] = H[c, rows, :].T

    each(0, 2, turn)

    def pass_on(c):
        def go(q):
            near_gather_in(q, c).wait_recv()
            across(near_slot(q, c)).start()
        each(1, 5, go)

    far_gather_in(0).wait_recv()
    opposite_gather().start()
    each(1, 5, lambda q: near_gather(q, 2).start())
    far_gather_in(1).wait_recv()
    each(1, 5, lambda q: near_gather(q, 1).start())

    each(1, NGX, lambda r: gather_in(r).wait_recv())
    MP[...] = nn(MG[...].reshape(NGX * PD, 256), jm).astype(BF16)

    def press(t):
        rows = pl.ds(pl.multiple_of(t * 256, 256), 256)
        p = nn(H[0, rows, :], MG[...].reshape(NGX * PD, 256)) + nn(H[1, rows, :], MP[...])
        PB[lax.div(t, 2), pl.ds(lax.rem(t, 2) * 8, 8)] = p.astype(BF16).reshape(8, PD, 256)

    each(0, 4, press)

    def start_parts(q):
        for c in (1, 2, 0):
            near_part(q, c).start()

    opposite_part().start()
    each(1, 5, start_parts)
    start_crossing()
    across(NZ - FAR).start()
    across(FAR).start()
    pass_on(0)

    each(2, 4, turn)

    def local_forward(b):
        bx, by = lax.div(b, 2), lax.rem(b, 2)
        m = b * 5
        x = X[bx, by]
        own = nt(x, C[m, 0]) + times_i(nt(x, C[m, 1]))
        OWN[bx, by] = own
        dx, dy = 1 - bx, 3 - by
        fx, fy = link(bx, by, dx), link(bx, by, dy)
        xs, ys = X[1 - bx, by], X[bx, 1 - by]
        re = fx * nt(xs, C[m + 1 + dx, 0]) + fy * nt(ys, C[m + 1 + dy, 0])
        im = fx * nt(xs, C[m + 1 + dx, 1]) + fy * nt(ys, C[m + 1 + dy, 1])
        RES[bx, by] = own + re + times_i(im) - E[bx, by].astype(F32)

    def local_adjoint(b):
        bx, by = lax.div(b, 2), lax.rem(b, 2)
        MULT[bx, by] = (
            back(bx, by, 0)
            + link(1 - bx, by, bx) * back(1 - bx, by, 1 + bx)
            + link(bx, 1 - by, 2 + by) * back(bx, 1 - by, 3 + by))


    opposite_gather_in().wait_recv()
    across(8).start()

    pass_on(2)
    pass_on(1)
    start_halos(1)

    def turn_loads(k):
        LP[k] = nn(LG[pl.ds(k * 8, 8)].reshape(256, 256), jm).astype(BF16)

    def react(y, t):
        rows = pl.ds(pl.multiple_of(t * 256, 256), 256)
        total = jnp.zeros((256, 256), F32)
        for i in range(2):
            k = 2 * y + i
            total = total + nn(HT[0, k, rows, :], LG[pl.ds(k * 8, 8)].reshape(256, 256))
            total = total - nn(HT[1, k, rows, :], LP[k])
        return total.reshape(8, PD, 256)

    def react_own(t):
        QB[pl.ds(t * 8, 8)] = react(yh, t)

    def react_other(t):
        rows = pl.ds(t * 8, 8)
        QB[rows] = QB[rows] + react(1 - yh, t)

    each(2 * yh, 2 * yh + 2, turn_loads)
    each(0, 2, react_own)
    each(0, NZ, lambda o: across_in(o).wait_recv())
    each(2 - 2 * yh, 4 - 2 * yh, turn_loads)
    each(0, 2, react_other)
    each(1, NGX, lambda r: sum_part(r).start())

    def done_parts(q):
        for c in range(3):
            near_part(q, c).wait_recv()

    opposite_part().wait_recv()
    each(1, 5, done_parts)

    for c in range(3):
        total = PB[:, lax.rem(z + CHUNKS[c], NZ)].astype(F32)
        for q in range(0 if c == 1 else 1, 5):
            total = total + RA[q, c if q else 0].astype(F32)
        T[c] = total
    for i, (c, dy) in enumerate(((0, 1), (1, 0), (2, 0), (1, 1), (2, 1))):
        TB[i] = T[c, lax.rem(yh + dy, 2)].astype(BF16)
    for i in (4, 3, 2, 1, 0):
        far_part(i).start()
    loads[5].wait()
    each(0, 4, local_forward)
    each(0, 4, local_adjoint)

    wait_halos(0)

    def halo_forward(b):
        bx, by = lax.div(b, 2), lax.rem(b, 2)
        m = b * 5 + 1
        fx = link(bx, by, bx) * edge_x(bx)
        fy = link(bx, by, 2 + by) * edge_y(by)
        xs = jnp.where(edge_x(bx) > 0.5, HX[bx, by], jnp.zeros((256, 128), BF16))
        ys = jnp.where(edge_y(by) > 0.5, HY[by, bx], jnp.zeros((256, 128), BF16))
        re = fx * nt(xs, C[m + bx, 0]) + fy * nt(ys, C[m + 2 + by, 0])
        im = fx * nt(xs, C[m + bx, 1]) + fy * nt(ys, C[m + 2 + by, 1])
        RES[bx, by] = RES[bx, by] + re + times_i(im)

    each(0, 4, halo_forward)
    wait_halos(1)

    def halo_adjoint(b):
        bx, by = lax.div(b, 2), lax.rem(b, 2)
        xs = jnp.where(edge_x(bx) > 0.5, RX[bx, by].astype(F32), 0.0)
        ys = jnp.where(edge_y(by) > 0.5, RY[by, bx].astype(F32), 0.0)
        MULT[bx, by] = MULT[bx, by] + xs + ys

    each(0, 4, halo_adjoint)

    for i in range(2):
        far_gather(i).wait_send()
        sent_halos(i)
    opposite_gather().wait_send()
    opposite_part().wait_send()
    each(1, NGX, lambda r: gather(r).wait_send())
    each(0, NZ, lambda o: across(o).wait_send())

    def sent_near(q):
        for c in range(3):
            near_gather(q, c).wait_send()
            near_part(q, c).wait_send()

    each(1, 5, sent_near)

    each(1, NGX, lambda r: sum_part(r).wait_recv())
    total = QB[gx]
    for r in range(1, NGX):
        total = total + RG[r]
    reaction_o[...] = total.astype(BF16)

    total = T[0, yh]
    for i in range(5):
        far_part(i).wait_recv()
        total = total + RB[i].astype(F32)
    pressure_o[...] = total

    each(1, NGX, lambda r: sum_part(r).wait_send())
    for i in range(5):
        far_part(i).wait_send()


def finish(lift, scale, pressure, reaction, pmap, res_in, mult_in, own, res_h, mult_h, sens_o,
           res_v, mult_v, sem):
    p = pressure[...]
    high = p.astype(BF16)
    low = (p - high.astype(F32)).astype(BF16)
    copies = []
    for b in range(4):
        at = (b // 2, b % 2)
        m = pmap[:, b * 128:(b + 1) * 128]
        mult = mult_in[at] + lift * tn(reaction[...], m)
        mult_v[at] = mult
        copies.append(pltpu.make_async_copy(mult_v.at[at], mult_h.at[at], sem.at[0, b]))
        copies[-1].start()
        res_v[at] = res_in[at] + lift * (tn(high, m) + tn(low, m))
        copies.append(pltpu.make_async_copy(res_v.at[at], res_h.at[at], sem.at[1, b]))
        copies[-1].start()
        sens_o[at] = jnp.sum(mult * own[at]) * scale
    for c in copies:
        c.wait()


def on_device(plate_motion, adjoint_load, excitation, coupling, joints, hydro, panel_map):
    lift = math.sqrt(4 * 128 / PD)
    hbm = pl.BlockSpec(memory_space=pltpu.HBM)
    vm = pl.BlockSpec(memory_space=pltpu.VMEM)
    sm = pl.BlockSpec(memory_space=pltpu.SMEM)
    block = (2, 2, 256, 128)
    panel = (PD, 256)
    dma = pltpu.SemaphoreType.DMA
    whole = jax.ShapeDtypeStruct(block, F32)
    res, mult, own, pressure, reaction, pmap = pl.pallas_call(
        kernel,
        out_shape=(
            whole, whole, whole,
            jax.ShapeDtypeStruct(panel, F32),
            jax.ShapeDtypeStruct(panel, BF16),
            jax.ShapeDtypeStruct((PD, 512), BF16),
        ),
        in_specs=[hbm] * 7,
        out_specs=(vm,) * 6,
        scratch_shapes=[
            pltpu.VMEM(block, BF16),
            pltpu.VMEM(block, BF16),
            pltpu.VMEM(block, BF16),
            pltpu.VMEM(block, BF16),
            pltpu.VMEM((20, 2, 128, 128), BF16),
            pltpu.VMEM((2, 1024, 512), BF16),
            pltpu.VMEM((2, 4, 512, 256), BF16),
            pltpu.VMEM((128, 128), BF16),
            pltpu.VMEM((128, 128), F32),
            pltpu.VMEM((NGX,) + panel, BF16),
            pltpu.VMEM((NGX * PD, 256), BF16),
            pltpu.VMEM((NGY,) + panel, BF16),
            pltpu.VMEM((4, 256, 256), BF16),
            pltpu.VMEM((2, NZ) + panel, BF16),
            pltpu.VMEM((5, 3, 2) + panel, BF16),
            pltpu.VMEM((3, 2) + panel, F32),
            pltpu.VMEM((5,) + panel, BF16),
            pltpu.VMEM((5,) + panel, BF16),
            pltpu.VMEM((NGX,) + panel, F32),
            pltpu.VMEM((NGX,) + panel, F32),
            pltpu.VMEM(block, BF16),
            pltpu.VMEM(block, BF16),
            pltpu.VMEM(block, BF16),
            pltpu.VMEM(block, BF16),
            pltpu.VMEM(block, BF16),
            pltpu.VMEM(block, BF16),
            pltpu.SMEM((2, 2, 4), jnp.int32),
            dma((7,)),
            dma((NGX,)), dma((NGX,)),
            dma((2,)), dma((2,)),
            dma((5, 3)), dma((5, 3)),
            dma((NZ,)), dma((NZ,)),
            dma((5, 3)), dma((5, 3)),
            dma((5,)), dma((5,)),
            dma((NGX,)), dma((NGX,)),
            dma((4, 2)), dma((4, 2)),
        ],
        compiler_params=pltpu.CompilerParams(
            collective_id=0, has_side_effects=True, vmem_limit_bytes=32 << 20),
        name="plate",
    )(
        *(pltpu.with_memory_space_constraint(x, pltpu.HBM) for x in (
            joints,
            plate_motion.reshape(block),
            adjoint_load.reshape(block),
            excitation.reshape(block),
            coupling.reshape(20, 2, 128, 128),
            hydro,
            panel_map.reshape(128, 128))),
    )
    res, mult, sens = pl.pallas_call(
        functools.partial(finish, lift, 1.0 / 128.0),
        out_shape=(whole, whole, jax.ShapeDtypeStruct((2, 2), F32)),
        in_specs=[vm] * 6,
        out_specs=(hbm, hbm, sm),
        scratch_shapes=[pltpu.VMEM(block, F32)] * 2 + [dma((2, 4))],
        compiler_params=pltpu.CompilerParams(vmem_limit_bytes=32 << 20),
        name="finish",
    )(pressure, reaction, pmap, res, mult, own)
    shape = plate_motion.shape
    return res.reshape(shape), mult.reshape(shape), sens


def solution(mesh):
    placed = (
        P("gx", "gy", None, None, None),
        P("gx", "gy", None, None, None),
        P("gx", "gy", None, None, None),
        P("gx", "gy", None, None, None, None),
        P("gx", "gy", None),
        P(None, "gx", "gy"),
        P(("gx", "gy"), None, None, None),
    )
    return jax.shard_map(
        on_device,
        mesh=mesh,
        in_specs=placed,
        out_specs=(P("gx", "gy", None, None, None), P("gx", "gy", None, None, None), P("gx", "gy")),
        check_vma=False,
    )
```

```python
import functools
import math

import jax
import jax.numpy as jnp
from jax import lax
from jax.experimental import pallas as pl
from jax.experimental.pallas import tpu as pltpu
from jax.sharding import PartitionSpec as P

MESH = pl.DeviceIdType.MESH
F32 = jnp.float32
BF16 = jnp.bfloat16
NGX, NGY, NZ = 16, 32, 16
PD = 32
FAR = 5
CHUNKS = (0, FAR, NZ - FAR)


def nn(a, b):
    return jnp.dot(a, b, preferred_element_type=F32)


def nt(a, b):
    return lax.dot_general(a, b, (((1,), (1,)), ((), ())), preferred_element_type=F32)


def tn(a, b):
    return lax.dot_general(a, b, (((0,), (0,)), ((), ())), preferred_element_type=F32)


def times_i(x):
    rows = x.shape[0]
    even = lax.rem(lax.broadcasted_iota(jnp.int32, x.shape, 0), 2) == 0
    return jnp.where(even, -pltpu.roll(x, rows - 1, 0), pltpu.roll(x, 1, 0))


def lane_i(width):
    r = lax.broadcasted_iota(jnp.int32, (width, width), 0)
    c = lax.broadcasted_iota(jnp.int32, (width, width), 1)
    odd = lax.rem(c, 2) == 1
    plus = jnp.where(jnp.logical_and(odd, r == c - 1), 1.0, 0.0)
    minus = jnp.where(jnp.logical_and(jnp.logical_not(odd), r == c + 1), 1.0, 0.0)
    return (plus - minus).astype(BF16)


def kernel(
    joints_h, plate_h, adj_h, exc_h, coup_h, hyd_h, pmap_h,
    RES, MULT, OWN, pressure_o, reaction_o, map_o,
    X, A, JA, E, C, H, HT, PM, PM32, MG, MP, LG, LP, PB, RA, T, TB, RB, QB, QC, QS, RG,
    HX, HY, TX, TY, RX, RY, joints,
    lsem, gx_s, gx_r, fa_s, fa_r, nb_s, nb_r, yf_s, yf_r,
    ra_s, ra_r, rb_s, rb_r, rc_s, rc_r, rx_s, rx_r, h_s, h_r,
):
    gx = lax.axis_index("gx")
    gy = lax.axis_index("gy")
    yh = lax.div(gy, NZ)
    z = lax.rem(gy, NZ)

    def gx_at(r):
        return lax.rem(gx + r, NGX)

    def gy_at(dz, dy):
        return lax.rem(yh + dy, 2) * NZ + lax.rem(z + dz, NZ)

    def near(q):
        return lax.rem(lax.rem(q + 2, 5) - 2 + NZ, NZ)

    def each(lo, hi, f):
        def body(i, carry):
            f(i)
            return carry
        lax.fori_loop(lo, hi, body, 0)

    def remote(src, dst, send, recv, where):
        return pltpu.make_async_remote_copy(
            src, dst, send, recv, device_id=where, device_id_type=MESH)

    loads = [
        pltpu.make_async_copy(s, d, lsem.at[i])
        for i, (s, d) in enumerate(
            ((pmap_h, PM), (adj_h, A), (plate_h, X), (coup_h, C), (hyd_h, H), (exc_h, E),
             (joints_h, joints))
        )
    ]
    for c in loads:
        c.start()

    bar = pltpu.get_barrier_semaphore()

    def greet(x, y):
        pl.semaphore_signal(bar, inc=1, device_id=(x, y), device_id_type=MESH)

    for dz in (FAR, NZ - FAR, 3, NZ - 3):
        greet(gx, gy_at(dz, 0))
    greet(gx, gy_at(0, 1))
    for step in (1, NGY - 1):
        greet(gx, lax.rem(gy + step, NGY))
    each(1, 5, lambda q: greet(gx, gy_at(near(q), 0)))
    each(1, NGX, lambda r: greet(gx_at(r), gy))

    def far_gather(i):
        return remote(LG.at[gy], LG.at[gy], fa_s.at[i], fa_r.at[i],
                      (gx, gy_at((FAR, NZ - FAR)[i], 0)))

    def far_gather_in(i):
        slot = gy_at((NZ - FAR, FAR)[i], 0)
        return remote(LG.at[slot], LG.at[slot], fa_s.at[i], fa_r.at[i], (gx, slot))

    def gather(r):
        return remote(MG.at[gx], MG.at[gx], gx_s.at[r], gx_r.at[r], (gx_at(r), gy))

    def gather_in(r):
        slot = gx_at(NGX - r)
        return remote(MG.at[slot], MG.at[slot], gx_s.at[r], gx_r.at[r], (slot, gy))

    def near_gather(q, c):
        slot = gy_at(CHUNKS[c], 0)
        return remote(LG.at[slot], LG.at[slot], nb_s.at[q, c], nb_r.at[q, c],
                      (gx, gy_at(near(q), 0)))

    def near_slot(q, c):
        return lax.rem(NZ - near(q) + CHUNKS[c], NZ)

    def near_gather_in(q, c):
        slot = gy_at(near_slot(q, c), 0)
        return remote(LG.at[slot], LG.at[slot], nb_s.at[q, c], nb_r.at[q, c], (gx, slot))

    def opposite_gather():
        slot = gy_at(NZ - FAR, 0)
        return remote(LG.at[slot], LG.at[slot], nb_s.at[0, 0], nb_r.at[0, 0], (gx, gy_at(3, 0)))

    def opposite_gather_in():
        slot = gy_at(8, 0)
        return remote(LG.at[slot], LG.at[slot], nb_s.at[0, 0], nb_r.at[0, 0], (gx, slot))

    def across(o):
        slot = gy_at(o, 0)
        return remote(LG.at[slot], LG.at[slot], yf_s.at[o], yf_r.at[o], (gx, gy_at(0, 1)))

    def across_in(o):
        slot = gy_at(o, 1)
        return remote(LG.at[slot], LG.at[slot], yf_s.at[o], yf_r.at[o], (gx, gy_at(0, 1)))

    def near_part(q, c):
        return remote(PB.at[:, lax.rem(z + near(q) + CHUNKS[c], NZ)], RA.at[q, c],
                      ra_s.at[q, c], ra_r.at[q, c], (gx, gy_at(near(q), 0)))

    def opposite_part():
        return remote(PB.at[:, lax.rem(z + 8, NZ)], RA.at[0, 0],
                      ra_s.at[0, 0], ra_r.at[0, 0], (gx, gy_at(3, 0)))

    def far_part(i):
        dz, dy = ((0, 1), (FAR, 0), (NZ - FAR, 0), (FAR, 1), (NZ - FAR, 1))[i]
        return remote(TB.at[i], RB.at[i], rb_s.at[i], rb_r.at[i], (gx, gy_at(dz, dy)))

    core = lax.rem(gx, 2)
    chip = lax.div(gx, 2)

    def chip_at(r):
        return lax.rem(chip + r, NGX // 2)

    def core_part(t):
        rows = pl.ds(t * 4, 4)
        return remote(QB.at[rows, 1 - core], QC.at[rows], rc_s.at[t], rc_r.at[t],
                      (gx + 1 - 2 * core, gy))

    def sum_part(r):
        return remote(QS.at[chip_at(r)], RG.at[r], rx_s.at[r], rx_r.at[r],
                      (2 * chip_at(r) + core, gy))

    def side(gap, s):
        return gap if s else -gap

    def halo_x(src, dst, k, s):
        return remote(src.at[s], dst.at[1 - s], h_s.at[k, s], h_r.at[k, 1 - s],
                      (gx + side(1, s), gy))

    def halo_x_in(src, dst, k, s):
        return remote(src.at[s], dst.at[s], h_s.at[k, s], h_r.at[k, s], (gx + side(1, s), gy))

    def halo_y(src, dst, k, s):
        return remote(src.at[:, s] if k == 1 else src.at[s], dst.at[1 - s],
                      h_s.at[k, s], h_r.at[k, 1 - s], (gx, gy + side(1, s)))

    def halo_y_in(src, dst, k, s):
        return remote(src.at[:, s] if k == 1 else src.at[s], dst.at[s],
                      h_s.at[k, s], h_r.at[k, s], (gx, gy + side(1, s)))

    loads[0].wait()
    PM32[...] = PM[...].astype(F32)
    for b in range(4):
        map_o[:, b * 128:(b + 1) * 128] = PM32[pl.ds(b, PD, stride=4), :].astype(BF16)

    def panels(V):
        total = nt(map_o[:, 0:128], V[0, 0])
        for b in range(1, 4):
            total = total + nt(map_o[:, b * 128:(b + 1) * 128], V[b // 2, b % 2])
        return total.astype(BF16)

    loads[1].wait()
    LG[gy] = panels(A)
    loads[2].wait()
    MG[gx] = panels(X)

    loads[3].wait()
    loads[6].wait()

    def link(bx, by, d):
        return joints[bx, by, d].astype(F32)

    def edge_x(bx):
        v = gx + 2 * bx - 1
        return jnp.where(jnp.logical_and(v >= 0, v < NGX), 1.0, 0.0).astype(F32)

    def edge_y(by):
        v = gy + 2 * by - 1
        return jnp.where(jnp.logical_and(v >= 0, v < NGY), 1.0, 0.0).astype(F32)

    def back(bx, by, d):
        m = (bx * 2 + by) * 5 + d
        return nn(A[bx, by], C[m, 0]) - nn(JA[bx, by], C[m, 1])

    def outgoing(b):
        bx, by = lax.div(b, 2), lax.rem(b, 2)
        JA[bx, by] = times_i(A[bx, by].astype(F32)).astype(BF16)
        TX[bx, by] = (link(bx, by, bx) * edge_x(bx) * back(bx, by, 1 + bx)).astype(BF16)
        TY[by, bx] = (link(bx, by, 2 + by) * edge_y(by) * back(bx, by, 3 + by)).astype(BF16)

    each(0, 4, outgoing)
    def to_x(s):
        return gx + 1 < NGX if s else gx > 0

    def to_y(s):
        return gy + 1 < NGY if s else gy > 0

    def sent_halos(s):
        @pl.when(to_x(s))
        def _():
            halo_x(X, HX, 0, s).wait_send()
            halo_x(TX, RX, 2, s).wait_send()

        @pl.when(to_y(s))
        def _():
            halo_y(X, HY, 1, s).wait_send()
            halo_y(TY, RY, 3, s).wait_send()

    def crosses(s):
        return z == NZ - 1 if s else z == 0

    def start_crossing(k):
        for s in range(2):
            @pl.when(jnp.logical_and(to_y(s), crosses(s)))
            def _():
                halo_y(*((X, HY), (TY, RY))[k], 2 * k + 1, s).start()

    def start_halos(k):
        for s in range(2):
            @pl.when(to_x(s))
            def _():
                halo_x(*((X, HX), (TX, RX))[k], 2 * k, s).start()

            @pl.when(jnp.logical_and(to_y(s), jnp.logical_not(crosses(s))))
            def _():
                halo_y(*((X, HY), (TY, RY))[k], 2 * k + 1, s).start()

    def wait_halos(k):
        for s in range(2):
            @pl.when(to_x(s))
            def _():
                src, dst = ((X, HX), (TX, RX))[k]
                halo_x_in(src, dst, 2 * k, s).wait_recv()

            @pl.when(to_y(s))
            def _():
                src, dst = ((X, HY), (TY, RY))[k]
                halo_y_in(src, dst, 2 * k + 1, s).wait_recv()

    pl.semaphore_wait(bar, 4 + 1 + 2 + 4 + 15)

    for i in range(2):
        far_gather(i).start()
    each(1, NGX, lambda r: gather(r).start())
    across(0).start()
    start_halos(0)
    each(1, 5, lambda q: near_gather(q, 0).start())

    loads[4].wait()
    jm = lane_i(256)

    def turn(t):
        rows = pl.ds(pl.multiple_of(t * 256, 256), 256)
        for c in range(2):
            HT[c, t] = H[c, rows, :].T

    each(0, 2, turn)

    def pass_on(c):
        def go(q):
            near_gather_in(q, c).wait_recv()
            across(near_slot(q, c)).start()
        each(1, 5, go)

    far_gather_in(0).wait_recv()
    opposite_gather().start()
    each(1, 5, lambda q: near_gather(q, 2).start())
    far_gather_in(1).wait_recv()
    each(1, 5, lambda q: near_gather(q, 1).start())

    each(1, NGX, lambda r: gather_in(r).wait_recv())
    MP[...] = nn(MG[...].reshape(NGX * PD, 256), jm).astype(BF16)

    def press(t):
        rows = pl.ds(pl.multiple_of(t * 256, 256), 256)
        p = nn(H[0, rows, :], MG[...].reshape(NGX * PD, 256)) + nn(H[1, rows, :], MP[...])
        PB[lax.div(t, 2), pl.ds(lax.rem(t, 2) * 8, 8)] = p.astype(BF16).reshape(8, PD, 256)

    each(0, 4, press)

    def start_parts(q):
        for c in (1, 2, 0):
            near_part(q, c).start()

    opposite_part().start()
    each(1, 5, start_parts)
    across(NZ - FAR).start()
    across(FAR).start()
    pass_on(0)

    each(2, 4, turn)

    def local_forward(b):
        bx, by = lax.div(b, 2), lax.rem(b, 2)
        m = b * 5
        x = X[bx, by]
        own = nt(x, C[m, 0]) + times_i(nt(x, C[m, 1]))
        OWN[bx, by] = own
        dx, dy = 1 - bx, 3 - by
        fx, fy = link(bx, by, dx), link(bx, by, dy)
        xs, ys = X[1 - bx, by], X[bx, 1 - by]
        re = fx * nt(xs, C[m + 1 + dx, 0]) + fy * nt(ys, C[m + 1 + dy, 0])
        im = fx * nt(xs, C[m + 1 + dx, 1]) + fy * nt(ys, C[m + 1 + dy, 1])
        RES[bx, by] = own + re + times_i(im) - E[bx, by].astype(F32)

    def local_adjoint(b):
        bx, by = lax.div(b, 2), lax.rem(b, 2)
        MULT[bx, by] = (
            back(bx, by, 0)
            + link(1 - bx, by, bx) * back(1 - bx, by, 1 + bx)
            + link(bx, 1 - by, 2 + by) * back(bx, 1 - by, 3 + by))


    opposite_gather_in().wait_recv()
    across(8).start()

    pass_on(2)
    pass_on(1)
    start_crossing(0)
    start_crossing(1)
    start_halos(1)

    def turn_loads(k):
        LP[k] = nn(LG[pl.ds(k * 8, 8)].reshape(256, 256), jm).astype(BF16)

    def react(y, t):
        rows = pl.ds(pl.multiple_of(t * 256, 256), 256)
        total = jnp.zeros((256, 256), F32)
        for i in range(2):
            k = 2 * y + i
            total = total + nn(HT[0, k, rows, :], LG[pl.ds(k * 8, 8)].reshape(256, 256))
            total = total - nn(HT[1, k, rows, :], LP[k])
        return total.reshape(4, 2, PD, 256)

    def react_own(t):
        QB[pl.ds(t * 4, 4)] = react(yh, t)

    def react_other(t):
        rows = pl.ds(t * 4, 4)
        QB[rows] = QB[rows] + react(1 - yh, t)
        core_part(t).start()

    each(2 * yh, 2 * yh + 2, turn_loads)
    each(0, 2, react_own)
    each(0, NZ, lambda o: across_in(o).wait_recv())
    each(2 - 2 * yh, 4 - 2 * yh, turn_loads)
    each(0, 2, react_other)

    def done_parts(q):
        for c in range(3):
            near_part(q, c).wait_recv()

    opposite_part().wait_recv()
    each(1, 5, done_parts)

    for c in range(3):
        total = PB[:, lax.rem(z + CHUNKS[c], NZ)].astype(F32)
        for q in range(0 if c == 1 else 1, 5):
            total = total + RA[q, c if q else 0].astype(F32)
        T[c] = total
    for i, (c, dy) in enumerate(((0, 1), (1, 0), (2, 0), (1, 1), (2, 1))):
        TB[i] = T[c, lax.rem(yh + dy, 2)].astype(BF16)
    for i in (4, 3, 2, 1, 0):
        far_part(i).start()
    for t in range(2):
        core_part(t).wait_recv()
    QS[...] = QB[:, core] + QC[...]
    each(1, NGX // 2, lambda r: sum_part(r).start())

    loads[5].wait()
    each(0, 4, local_forward)
    each(0, 4, local_adjoint)

    wait_halos(0)

    def halo_forward(b):
        bx, by = lax.div(b, 2), lax.rem(b, 2)
        m = b * 5 + 1
        fx = link(bx, by, bx) * edge_x(bx)
        fy = link(bx, by, 2 + by) * edge_y(by)
        xs = jnp.where(edge_x(bx) > 0.5, HX[bx, by], jnp.zeros((256, 128), BF16))
        ys = jnp.where(edge_y(by) > 0.5, HY[by, bx], jnp.zeros((256, 128), BF16))
        re = fx * nt(xs, C[m + bx, 0]) + fy * nt(ys, C[m + 2 + by, 0])
        im = fx * nt(xs, C[m + bx, 1]) + fy * nt(ys, C[m + 2 + by, 1])
        RES[bx, by] = RES[bx, by] + re + times_i(im)

    each(0, 4, halo_forward)
    wait_halos(1)

    def halo_adjoint(b):
        bx, by = lax.div(b, 2), lax.rem(b, 2)
        xs = jnp.where(edge_x(bx) > 0.5, RX[bx, by].astype(F32), 0.0)
        ys = jnp.where(edge_y(by) > 0.5, RY[by, bx].astype(F32), 0.0)
        MULT[bx, by] = MULT[bx, by] + xs + ys

    each(0, 4, halo_adjoint)

    for i in range(2):
        far_gather(i).wait_send()
        sent_halos(i)
    opposite_gather().wait_send()
    opposite_part().wait_send()
    each(1, NGX, lambda r: gather(r).wait_send())
    each(0, NZ, lambda o: across(o).wait_send())

    def sent_near(q):
        for c in range(3):
            near_gather(q, c).wait_send()
            near_part(q, c).wait_send()

    each(1, 5, sent_near)

    each(1, NGX // 2, lambda r: sum_part(r).wait_recv())
    total = QS[chip]
    for r in range(1, NGX // 2):
        total = total + RG[r]
    reaction_o[...] = total.astype(BF16)

    total = T[0, yh]
    for i in range(5):
        far_part(i).wait_recv()
        total = total + RB[i].astype(F32)
    pressure_o[...] = total

    each(1, NGX // 2, lambda r: sum_part(r).wait_send())
    for t in range(2):
        core_part(t).wait_send()
    for i in range(5):
        far_part(i).wait_send()


def finish(lift, scale, pressure, reaction, pmap, res_in, mult_in, own, res_h, mult_h, sens_o,
           res_v, mult_v, sem):
    p = pressure[...]
    high = p.astype(BF16)
    low = (p - high.astype(F32)).astype(BF16)
    copies = []
    for b in range(4):
        at = (b // 2, b % 2)
        m = pmap[:, b * 128:(b + 1) * 128]
        mult = mult_in[at] + lift * tn(reaction[...], m)
        mult_v[at] = mult
        copies.append(pltpu.make_async_copy(mult_v.at[at], mult_h.at[at], sem.at[0, b]))
        copies[-1].start()
        res_v[at] = res_in[at] + lift * (tn(high, m) + tn(low, m))
        copies.append(pltpu.make_async_copy(res_v.at[at], res_h.at[at], sem.at[1, b]))
        copies[-1].start()
        sens_o[at] = jnp.sum(mult * own[at]) * scale
    for c in copies:
        c.wait()


def on_device(plate_motion, adjoint_load, excitation, coupling, joints, hydro, panel_map):
    lift = math.sqrt(4 * 128 / PD)
    hbm = pl.BlockSpec(memory_space=pltpu.HBM)
    vm = pl.BlockSpec(memory_space=pltpu.VMEM)
    sm = pl.BlockSpec(memory_space=pltpu.SMEM)
    block = (2, 2, 256, 128)
    panel = (PD, 256)
    dma = pltpu.SemaphoreType.DMA
    whole = jax.ShapeDtypeStruct(block, F32)
    res, mult, own, pressure, reaction, pmap = pl.pallas_call(
        kernel,
        out_shape=(
            whole, whole, whole,
            jax.ShapeDtypeStruct(panel, F32),
            jax.ShapeDtypeStruct(panel, BF16),
            jax.ShapeDtypeStruct((PD, 512), BF16),
        ),
        in_specs=[hbm] * 7,
        out_specs=(vm,) * 6,
        scratch_shapes=[
            pltpu.VMEM(block, BF16),
            pltpu.VMEM(block, BF16),
            pltpu.VMEM(block, BF16),
            pltpu.VMEM(block, BF16),
            pltpu.VMEM((20, 2, 128, 128), BF16),
            pltpu.VMEM((2, 1024, 512), BF16),
            pltpu.VMEM((2, 4, 512, 256), BF16),
            pltpu.VMEM((128, 128), BF16),
            pltpu.VMEM((128, 128), F32),
            pltpu.VMEM((NGX,) + panel, BF16),
            pltpu.VMEM((NGX * PD, 256), BF16),
            pltpu.VMEM((NGY,) + panel, BF16),
            pltpu.VMEM((4, 256, 256), BF16),
            pltpu.VMEM((2, NZ) + panel, BF16),
            pltpu.VMEM((5, 3, 2) + panel, BF16),
            pltpu.VMEM((3, 2) + panel, F32),
            pltpu.VMEM((5,) + panel, BF16),
            pltpu.VMEM((5,) + panel, BF16),
            pltpu.VMEM((NGX // 2, 2) + panel, F32),
            pltpu.VMEM((NGX // 2,) + panel, F32),
            pltpu.VMEM((NGX // 2,) + panel, F32),
            pltpu.VMEM((NGX // 2,) + panel, F32),
            pltpu.VMEM(block, BF16),
            pltpu.VMEM(block, BF16),
            pltpu.VMEM(block, BF16),
            pltpu.VMEM(block, BF16),
            pltpu.VMEM(block, BF16),
            pltpu.VMEM(block, BF16),
            pltpu.SMEM((2, 2, 4), jnp.int32),
            dma((7,)),
            dma((NGX,)), dma((NGX,)),
            dma((2,)), dma((2,)),
            dma((5, 3)), dma((5, 3)),
            dma((NZ,)), dma((NZ,)),
            dma((5, 3)), dma((5, 3)),
            dma((5,)), dma((5,)),
            dma((2,)), dma((2,)),
            dma((NGX // 2,)), dma((NGX // 2,)),
            dma((4, 2)), dma((4, 2)),
        ],
        compiler_params=pltpu.CompilerParams(
            collective_id=0, has_side_effects=True, vmem_limit_bytes=32 << 20),
        name="plate",
    )(
        *(pltpu.with_memory_space_constraint(x, pltpu.HBM) for x in (
            joints,
            plate_motion.reshape(block),
            adjoint_load.reshape(block),
            excitation.reshape(block),
            coupling.reshape(20, 2, 128, 128),
            hydro,
            panel_map.reshape(128, 128))),
    )
    res, mult, sens = pl.pallas_call(
        functools.partial(finish, lift, 1.0 / 128.0),
        out_shape=(whole, whole, jax.ShapeDtypeStruct((2, 2), F32)),
        in_specs=[vm] * 6,
        out_specs=(hbm, hbm, sm),
        scratch_shapes=[pltpu.VMEM(block, F32)] * 2 + [dma((2, 4))],
        compiler_params=pltpu.CompilerParams(vmem_limit_bytes=32 << 20),
        name="finish",
    )(pressure, reaction, pmap, res, mult, own)
    shape = plate_motion.shape
    return res.reshape(shape), mult.reshape(shape), sens


def solution(mesh):
    placed = (
        P("gx", "gy", None, None, None),
        P("gx", "gy", None, None, None),
        P("gx", "gy", None, None, None),
        P("gx", "gy", None, None, None, None),
        P("gx", "gy", None),
        P(None, "gx", "gy"),
        P(("gx", "gy"), None, None, None),
    )
    return jax.shard_map(
        on_device,
        mesh=mesh,
        in_specs=placed,
        out_specs=(P("gx", "gy", None, None, None), P("gx", "gy", None, None, None), P("gx", "gy")),
        check_vma=False,
    )
```

```python
import functools
import math

import jax
import jax.numpy as jnp
from jax import lax
from jax.experimental import pallas as pl
from jax.experimental.pallas import tpu as pltpu
from jax.sharding import PartitionSpec as P

MESH = pl.DeviceIdType.MESH
F32 = jnp.float32
BF16 = jnp.bfloat16
NGX, NGY, NZ = 16, 32, 16
PD = 32
FAR = 5
CHUNKS = (0, FAR, NZ - FAR)


def nn(a, b):
    return jnp.dot(a, b, preferred_element_type=F32)


def nt(a, b):
    return lax.dot_general(a, b, (((1,), (1,)), ((), ())), preferred_element_type=F32)


def tn(a, b):
    return lax.dot_general(a, b, (((0,), (0,)), ((), ())), preferred_element_type=F32)


def times_i(x):
    rows = x.shape[0]
    even = lax.rem(lax.broadcasted_iota(jnp.int32, x.shape, 0), 2) == 0
    return jnp.where(even, -pltpu.roll(x, rows - 1, 0), pltpu.roll(x, 1, 0))


def lane_i(width):
    r = lax.broadcasted_iota(jnp.int32, (width, width), 0)
    c = lax.broadcasted_iota(jnp.int32, (width, width), 1)
    odd = lax.rem(c, 2) == 1
    plus = jnp.where(jnp.logical_and(odd, r == c - 1), 1.0, 0.0)
    minus = jnp.where(jnp.logical_and(jnp.logical_not(odd), r == c + 1), 1.0, 0.0)
    return (plus - minus).astype(BF16)


def kernel(
    joints_h, plate_h, adj_h, exc_h, coup_h, hyd_h, pmap_h,
    RES, MULT, OWN, pressure_o, reaction_o, map_o,
    X, A, JA, E, C, H, HT, PM, PM32, MG, MP, LG, LP, PB, RA, T, TB, RB, QB, QC, QS, RG,
    HX, HY, TX, TY, RX, RY, joints,
    lsem, gx_s, gx_r, fa_s, fa_r, nb_s, nb_r, yf_s, yf_r,
    ra_s, ra_r, rb_s, rb_r, rc_s, rc_r, rx_s, rx_r, h_s, h_r,
):
    gx = lax.axis_index("gx")
    gy = lax.axis_index("gy")
    yh = lax.div(gy, NZ)
    z = lax.rem(gy, NZ)

    def gx_at(r):
        return lax.rem(gx + r, NGX)

    def gy_at(dz, dy):
        return lax.rem(yh + dy, 2) * NZ + lax.rem(z + dz, NZ)

    def near(q):
        return lax.rem(lax.rem(q + 2, 5) - 2 + NZ, NZ)

    def each(lo, hi, f):
        def body(i, carry):
            f(i)
            return carry
        lax.fori_loop(lo, hi, body, 0)

    def remote(src, dst, send, recv, where):
        return pltpu.make_async_remote_copy(
            src, dst, send, recv, device_id=where, device_id_type=MESH)

    loads = [
        pltpu.make_async_copy(s, d, lsem.at[i])
        for i, (s, d) in enumerate(
            ((pmap_h, PM), (adj_h, A), (plate_h, X), (coup_h, C), (hyd_h, H), (exc_h, E),
             (joints_h, joints))
        )
    ]
    for c in loads:
        c.start()

    bar = pltpu.get_barrier_semaphore()

    def greet(x, y):
        pl.semaphore_signal(bar, inc=1, device_id=(x, y), device_id_type=MESH)

    for dz in (FAR, NZ - FAR, 3, NZ - 3):
        greet(gx, gy_at(dz, 0))
    greet(gx, gy_at(0, 1))
    for step in (1, NGY - 1):
        greet(gx, lax.rem(gy + step, NGY))
    each(1, 5, lambda q: greet(gx, gy_at(near(q), 0)))
    each(1, NGX, lambda r: greet(gx_at(r), gy))

    def far_gather(i):
        return remote(LG.at[gy], LG.at[gy], fa_s.at[i], fa_r.at[i],
                      (gx, gy_at((FAR, NZ - FAR)[i], 0)))

    def far_gather_in(i):
        slot = gy_at((NZ - FAR, FAR)[i], 0)
        return remote(LG.at[slot], LG.at[slot], fa_s.at[i], fa_r.at[i], (gx, slot))

    def gather(r):
        return remote(MG.at[gx], MG.at[gx], gx_s.at[r], gx_r.at[r], (gx_at(r), gy))

    def gather_in(r):
        slot = gx_at(NGX - r)
        return remote(MG.at[slot], MG.at[slot], gx_s.at[r], gx_r.at[r], (slot, gy))

    def near_gather(q, c):
        slot = gy_at(CHUNKS[c], 0)
        return remote(LG.at[slot], LG.at[slot], nb_s.at[q, c], nb_r.at[q, c],
                      (gx, gy_at(near(q), 0)))

    def near_slot(q, c):
        return lax.rem(NZ - near(q) + CHUNKS[c], NZ)

    def near_gather_in(q, c):
        slot = gy_at(near_slot(q, c), 0)
        return remote(LG.at[slot], LG.at[slot], nb_s.at[q, c], nb_r.at[q, c], (gx, slot))

    def opposite_gather():
        slot = gy_at(NZ - FAR, 0)
        return remote(LG.at[slot], LG.at[slot], nb_s.at[0, 0], nb_r.at[0, 0], (gx, gy_at(3, 0)))

    def opposite_gather_in():
        slot = gy_at(8, 0)
        return remote(LG.at[slot], LG.at[slot], nb_s.at[0, 0], nb_r.at[0, 0], (gx, slot))

    def across(o):
        slot = gy_at(o, 0)
        return remote(LG.at[slot], LG.at[slot], yf_s.at[o], yf_r.at[o], (gx, gy_at(0, 1)))

    def across_in(o):
        slot = gy_at(o, 1)
        return remote(LG.at[slot], LG.at[slot], yf_s.at[o], yf_r.at[o], (gx, gy_at(0, 1)))

    def near_part(q, c):
        return remote(PB.at[:, lax.rem(z + near(q) + CHUNKS[c], NZ)], RA.at[q, c],
                      ra_s.at[q, c], ra_r.at[q, c], (gx, gy_at(near(q), 0)))

    def opposite_part():
        return remote(PB.at[:, lax.rem(z + 8, NZ)], RA.at[0, 0],
                      ra_s.at[0, 0], ra_r.at[0, 0], (gx, gy_at(3, 0)))

    def far_part(i):
        dz, dy = ((0, 1), (FAR, 0), (NZ - FAR, 0), (FAR, 1), (NZ - FAR, 1))[i]
        return remote(TB.at[i], RB.at[i], rb_s.at[i], rb_r.at[i], (gx, gy_at(dz, dy)))

    core = lax.rem(gx, 2)
    chip = lax.div(gx, 2)

    def chip_at(r):
        return lax.rem(chip + r, NGX // 2)

    def core_part(t):
        rows = pl.ds(t * 4, 4)
        return remote(QB.at[rows, 1 - core], QC.at[rows], rc_s.at[t], rc_r.at[t],
                      (gx + 1 - 2 * core, gy))

    def sum_part(r):
        return remote(QS.at[chip_at(r)], RG.at[r], rx_s.at[r], rx_r.at[r],
                      (2 * chip_at(r) + core, gy))

    def side(gap, s):
        return gap if s else -gap

    def halo_x(src, dst, k, s):
        return remote(src.at[s], dst.at[1 - s], h_s.at[k, s], h_r.at[k, 1 - s],
                      (gx + side(1, s), gy))

    def halo_x_in(src, dst, k, s):
        return remote(src.at[s], dst.at[s], h_s.at[k, s], h_r.at[k, s], (gx + side(1, s), gy))

    def halo_y(src, dst, k, s):
        return remote(src.at[:, s] if k == 1 else src.at[s], dst.at[1 - s],
                      h_s.at[k, s], h_r.at[k, 1 - s], (gx, gy + side(1, s)))

    def halo_y_in(src, dst, k, s):
        return remote(src.at[:, s] if k == 1 else src.at[s], dst.at[s],
                      h_s.at[k, s], h_r.at[k, s], (gx, gy + side(1, s)))

    loads[0].wait()
    PM32[...] = PM[...].astype(F32)
    for b in range(4):
        map_o[:, b * 128:(b + 1) * 128] = PM32[pl.ds(b, PD, stride=4), :].astype(BF16)

    def panels(V):
        total = nt(map_o[:, 0:128], V[0, 0])
        for b in range(1, 4):
            total = total + nt(map_o[:, b * 128:(b + 1) * 128], V[b // 2, b % 2])
        return total.astype(BF16)

    loads[1].wait()
    LG[gy] = panels(A)
    loads[2].wait()
    MG[gx] = panels(X)


    def link(bx, by, d):
        return joints[bx, by, d].astype(F32)

    def edge_x(bx):
        v = gx + 2 * bx - 1
        return jnp.where(jnp.logical_and(v >= 0, v < NGX), 1.0, 0.0).astype(F32)

    def edge_y(by):
        v = gy + 2 * by - 1
        return jnp.where(jnp.logical_and(v >= 0, v < NGY), 1.0, 0.0).astype(F32)

    def back(bx, by, d):
        m = (bx * 2 + by) * 5 + d
        return nn(A[bx, by], C[m, 0]) - nn(JA[bx, by], C[m, 1])

    def outgoing(b):
        bx, by = lax.div(b, 2), lax.rem(b, 2)
        JA[bx, by] = times_i(A[bx, by].astype(F32)).astype(BF16)
        TX[bx, by] = (link(bx, by, bx) * edge_x(bx) * back(bx, by, 1 + bx)).astype(BF16)
        TY[by, bx] = (link(bx, by, 2 + by) * edge_y(by) * back(bx, by, 3 + by)).astype(BF16)

    def to_x(s):
        return gx + 1 < NGX if s else gx > 0

    def to_y(s):
        return gy + 1 < NGY if s else gy > 0

    def sent_halos(s):
        @pl.when(to_x(s))
        def _():
            halo_x(X, HX, 0, s).wait_send()
            halo_x(TX, RX, 2, s).wait_send()

        @pl.when(to_y(s))
        def _():
            halo_y(X, HY, 1, s).wait_send()
            halo_y(TY, RY, 3, s).wait_send()

    def crosses(s):
        return z == NZ - 1 if s else z == 0

    def start_crossing(k):
        for s in range(2):
            @pl.when(jnp.logical_and(to_y(s), crosses(s)))
            def _():
                halo_y(*((X, HY), (TY, RY))[k], 2 * k + 1, s).start()

    def start_halos(k):
        for s in range(2):
            @pl.when(to_x(s))
            def _():
                halo_x(*((X, HX), (TX, RX))[k], 2 * k, s).start()

            @pl.when(jnp.logical_and(to_y(s), jnp.logical_not(crosses(s))))
            def _():
                halo_y(*((X, HY), (TY, RY))[k], 2 * k + 1, s).start()

    def wait_halos(k):
        for s in range(2):
            @pl.when(to_x(s))
            def _():
                src, dst = ((X, HX), (TX, RX))[k]
                halo_x_in(src, dst, 2 * k, s).wait_recv()

            @pl.when(to_y(s))
            def _():
                src, dst = ((X, HY), (TY, RY))[k]
                halo_y_in(src, dst, 2 * k + 1, s).wait_recv()

    pl.semaphore_wait(bar, 4 + 1 + 2 + 4 + 15)

    for i in range(2):
        far_gather(i).start()
    each(1, NGX, lambda r: gather(r).start())
    across(0).start()
    start_halos(0)
    each(1, 5, lambda q: near_gather(q, 0).start())
    loads[3].wait()
    loads[6].wait()
    each(0, 4, outgoing)

    loads[4].wait()
    jm = lane_i(256)

    def turn(t):
        rows = pl.ds(pl.multiple_of(t * 256, 256), 256)
        for c in range(2):
            HT[c, t] = H[c, rows, :].T

    each(0, 2, turn)

    def pass_on(c):
        def go(q):
            near_gather_in(q, c).wait_recv()
            across(near_slot(q, c)).start()
        each(1, 5, go)

    far_gather_in(0).wait_recv()
    opposite_gather().start()
    each(1, 5, lambda q: near_gather(q, 2).start())
    far_gather_in(1).wait_recv()
    each(1, 5, lambda q: near_gather(q, 1).start())

    each(1, NGX, lambda r: gather_in(r).wait_recv())
    MP[...] = nn(MG[...].reshape(NGX * PD, 256), jm).astype(BF16)

    def press(t):
        rows = pl.ds(pl.multiple_of(t * 256, 256), 256)
        p = nn(H[0, rows, :], MG[...].reshape(NGX * PD, 256)) + nn(H[1, rows, :], MP[...])
        PB[lax.div(t, 2), pl.ds(lax.rem(t, 2) * 8, 8)] = p.astype(BF16).reshape(8, PD, 256)

    each(0, 4, press)

    def start_parts(q):
        for c in (1, 2, 0):
            near_part(q, c).start()

    opposite_part().start()
    each(1, 5, start_parts)
    across(NZ - FAR).start()
    across(FAR).start()
    pass_on(0)

    each(2, 4, turn)

    def local_forward(b):
        bx, by = lax.div(b, 2), lax.rem(b, 2)
        m = b * 5
        x = X[bx, by]
        own = nt(x, C[m, 0]) + times_i(nt(x, C[m, 1]))
        OWN[bx, by] = own
        dx, dy = 1 - bx, 3 - by
        fx, fy = link(bx, by, dx), link(bx, by, dy)
        xs, ys = X[1 - bx, by], X[bx, 1 - by]
        re = fx * nt(xs, C[m + 1 + dx, 0]) + fy * nt(ys, C[m + 1 + dy, 0])
        im = fx * nt(xs, C[m + 1 + dx, 1]) + fy * nt(ys, C[m + 1 + dy, 1])
        RES[bx, by] = own + re + times_i(im) - E[bx, by].astype(F32)

    def local_adjoint(b):
        bx, by = lax.div(b, 2), lax.rem(b, 2)
        MULT[bx, by] = (
            back(bx, by, 0)
            + link(1 - bx, by, bx) * back(1 - bx, by, 1 + bx)
            + link(bx, 1 - by, 2 + by) * back(bx, 1 - by, 3 + by))


    opposite_gather_in().wait_recv()
    across(8).start()

    pass_on(2)
    pass_on(1)
    start_crossing(0)
    start_crossing(1)
    start_halos(1)

    def turn_loads(k):
        LP[k] = nn(LG[pl.ds(k * 8, 8)].reshape(256, 256), jm).astype(BF16)

    def react(y, t):
        rows = pl.ds(pl.multiple_of(t * 256, 256), 256)
        total = jnp.zeros((256, 256), F32)
        for i in range(2):
            k = 2 * y + i
            total = total + nn(HT[0, k, rows, :], LG[pl.ds(k * 8, 8)].reshape(256, 256))
            total = total - nn(HT[1, k, rows, :], LP[k])
        return total.reshape(4, 2, PD, 256)

    def react_own(t):
        QB[pl.ds(t * 4, 4)] = react(yh, t)

    def react_other(t):
        rows = pl.ds(t * 4, 4)
        QB[rows] = QB[rows] + react(1 - yh, t)
        core_part(t).start()

    each(2 * yh, 2 * yh + 2, turn_loads)
    each(0, 2, react_own)
    each(0, NZ, lambda o: across_in(o).wait_recv())
    each(2 - 2 * yh, 4 - 2 * yh, turn_loads)
    each(0, 2, react_other)

    def done_parts(q):
        for c in range(3):
            near_part(q, c).wait_recv()

    opposite_part().wait_recv()
    each(1, 5, done_parts)

    for c in range(3):
        total = PB[:, lax.rem(z + CHUNKS[c], NZ)].astype(F32)
        for q in range(0 if c == 1 else 1, 5):
            total = total + RA[q, c if q else 0].astype(F32)
        T[c] = total
    for i, (c, dy) in enumerate(((0, 1), (1, 0), (2, 0), (1, 1), (2, 1))):
        TB[i] = T[c, lax.rem(yh + dy, 2)].astype(BF16)
    for i in (4, 3, 2, 1, 0):
        far_part(i).start()
    for t in range(2):
        core_part(t).wait_recv()
    QS[...] = QB[:, core] + QC[...]
    each(1, NGX // 2, lambda r: sum_part(r).start())

    loads[5].wait()
    each(0, 4, local_forward)
    each(0, 4, local_adjoint)

    wait_halos(0)

    def halo_forward(b):
        bx, by = lax.div(b, 2), lax.rem(b, 2)
        m = b * 5 + 1
        fx = link(bx, by, bx) * edge_x(bx)
        fy = link(bx, by, 2 + by) * edge_y(by)
        xs = jnp.where(edge_x(bx) > 0.5, HX[bx, by], jnp.zeros((256, 128), BF16))
        ys = jnp.where(edge_y(by) > 0.5, HY[by, bx], jnp.zeros((256, 128), BF16))
        re = fx * nt(xs, C[m + bx, 0]) + fy * nt(ys, C[m + 2 + by, 0])
        im = fx * nt(xs, C[m + bx, 1]) + fy * nt(ys, C[m + 2 + by, 1])
        RES[bx, by] = RES[bx, by] + re + times_i(im)

    each(0, 4, halo_forward)
    wait_halos(1)

    def halo_adjoint(b):
        bx, by = lax.div(b, 2), lax.rem(b, 2)
        xs = jnp.where(edge_x(bx) > 0.5, RX[bx, by].astype(F32), 0.0)
        ys = jnp.where(edge_y(by) > 0.5, RY[by, bx].astype(F32), 0.0)
        MULT[bx, by] = MULT[bx, by] + xs + ys

    each(0, 4, halo_adjoint)

    for i in range(2):
        far_gather(i).wait_send()
        sent_halos(i)
    opposite_gather().wait_send()
    opposite_part().wait_send()
    each(1, NGX, lambda r: gather(r).wait_send())
    each(0, NZ, lambda o: across(o).wait_send())

    def sent_near(q):
        for c in range(3):
            near_gather(q, c).wait_send()
            near_part(q, c).wait_send()

    each(1, 5, sent_near)

    each(1, NGX // 2, lambda r: sum_part(r).wait_recv())
    total = QS[chip]
    for r in range(1, NGX // 2):
        total = total + RG[r]
    reaction_o[...] = total.astype(BF16)

    total = T[0, yh]
    for i in range(5):
        far_part(i).wait_recv()
        total = total + RB[i].astype(F32)
    pressure_o[...] = total

    each(1, NGX // 2, lambda r: sum_part(r).wait_send())
    for t in range(2):
        core_part(t).wait_send()
    for i in range(5):
        far_part(i).wait_send()


def finish(lift, scale, pressure, reaction, pmap, res_in, mult_in, own, res_h, mult_h, sens_o,
           res_v, mult_v, sem):
    p = pressure[...]
    high = p.astype(BF16)
    low = (p - high.astype(F32)).astype(BF16)
    m = pmap[...]
    mult_force = lift * tn(reaction[...], m)
    res_force = lift * tn(jnp.concatenate([high, low]), jnp.concatenate([m, m]))
    copies = []
    for b in range(4):
        at = (b // 2, b % 2)
        lanes = slice(b * 128, (b + 1) * 128)
        for i, (force, src, buf, out) in enumerate((
                (mult_force, mult_in, mult_v, mult_h), (res_force, res_in, res_v, res_h))):
            buf[at] = src[at] + force[:, lanes]
            copies.append(pltpu.make_async_copy(buf.at[at], out.at[at], sem.at[i, b]))
            copies[-1].start()
    for b in range(4):
        at = (b // 2, b % 2)
        sens_o[at] = jnp.sum(mult_v[at] * own[at]) * scale
    for c in copies:
        c.wait()


def on_device(plate_motion, adjoint_load, excitation, coupling, joints, hydro, panel_map):
    lift = math.sqrt(4 * 128 / PD)
    hbm = pl.BlockSpec(memory_space=pltpu.HBM)
    vm = pl.BlockSpec(memory_space=pltpu.VMEM)
    sm = pl.BlockSpec(memory_space=pltpu.SMEM)
    block = (2, 2, 256, 128)
    panel = (PD, 256)
    dma = pltpu.SemaphoreType.DMA
    whole = jax.ShapeDtypeStruct(block, F32)
    res, mult, own, pressure, reaction, pmap = pl.pallas_call(
        kernel,
        out_shape=(
            whole, whole, whole,
            jax.ShapeDtypeStruct(panel, F32),
            jax.ShapeDtypeStruct(panel, BF16),
            jax.ShapeDtypeStruct((PD, 512), BF16),
        ),
        in_specs=[hbm] * 7,
        out_specs=(vm,) * 6,
        scratch_shapes=[
            pltpu.VMEM(block, BF16),
            pltpu.VMEM(block, BF16),
            pltpu.VMEM(block, BF16),
            pltpu.VMEM(block, BF16),
            pltpu.VMEM((20, 2, 128, 128), BF16),
            pltpu.VMEM((2, 1024, 512), BF16),
            pltpu.VMEM((2, 4, 512, 256), BF16),
            pltpu.VMEM((128, 128), BF16),
            pltpu.VMEM((128, 128), F32),
            pltpu.VMEM((NGX,) + panel, BF16),
            pltpu.VMEM((NGX * PD, 256), BF16),
            pltpu.VMEM((NGY,) + panel, BF16),
            pltpu.VMEM((4, 256, 256), BF16),
            pltpu.VMEM((2, NZ) + panel, BF16),
            pltpu.VMEM((5, 3, 2) + panel, BF16),
            pltpu.VMEM((3, 2) + panel, F32),
            pltpu.VMEM((5,) + panel, BF16),
            pltpu.VMEM((5,) + panel, BF16),
            pltpu.VMEM((NGX // 2, 2) + panel, F32),
            pltpu.VMEM((NGX // 2,) + panel, F32),
            pltpu.VMEM((NGX // 2,) + panel, F32),
            pltpu.VMEM((NGX // 2,) + panel, F32),
            pltpu.VMEM(block, BF16),
            pltpu.VMEM(block, BF16),
            pltpu.VMEM(block, BF16),
            pltpu.VMEM(block, BF16),
            pltpu.VMEM(block, BF16),
            pltpu.VMEM(block, BF16),
            pltpu.SMEM((2, 2, 4), jnp.int32),
            dma((7,)),
            dma((NGX,)), dma((NGX,)),
            dma((2,)), dma((2,)),
            dma((5, 3)), dma((5, 3)),
            dma((NZ,)), dma((NZ,)),
            dma((5, 3)), dma((5, 3)),
            dma((5,)), dma((5,)),
            dma((2,)), dma((2,)),
            dma((NGX // 2,)), dma((NGX // 2,)),
            dma((4, 2)), dma((4, 2)),
        ],
        compiler_params=pltpu.CompilerParams(
            collective_id=0, has_side_effects=True, vmem_limit_bytes=32 << 20),
        name="plate",
    )(
        *(pltpu.with_memory_space_constraint(x, pltpu.HBM) for x in (
            joints,
            plate_motion.reshape(block),
            adjoint_load.reshape(block),
            excitation.reshape(block),
            coupling.reshape(20, 2, 128, 128),
            hydro,
            panel_map.reshape(128, 128))),
    )
    res, mult, sens = pl.pallas_call(
        functools.partial(finish, lift, 1.0 / 128.0),
        out_shape=(whole, whole, jax.ShapeDtypeStruct((2, 2), F32)),
        in_specs=[vm] * 6,
        out_specs=(hbm, hbm, sm),
        scratch_shapes=[pltpu.VMEM(block, F32)] * 2 + [dma((2, 4))],
        compiler_params=pltpu.CompilerParams(vmem_limit_bytes=32 << 20),
        name="finish",
    )(pressure, reaction, pmap, res, mult, own)
    shape = plate_motion.shape
    return res.reshape(shape), mult.reshape(shape), sens


def solution(mesh):
    placed = (
        P("gx", "gy", None, None, None),
        P("gx", "gy", None, None, None),
        P("gx", "gy", None, None, None),
        P("gx", "gy", None, None, None, None),
        P("gx", "gy", None),
        P(None, "gx", "gy"),
        P(("gx", "gy"), None, None, None),
    )
    return jax.shard_map(
        on_device,
        mesh=mesh,
        in_specs=placed,
        out_specs=(P("gx", "gy", None, None, None), P("gx", "gy", None, None, None), P("gx", "gy")),
        check_vma=False,
    )
```
